512 devices in a mesh: row: 4 (over x), col: 8 (over y, core), layer: 16 (over z).
Axes of the slice: x: 4, y: 4, z: 16, core: 2. Of those that a mesh axis runs over, the one named last changes fastest.
Arguments:
- a_blocks: bfloat16 [16, 2, 64, 64, 512], P('layer', None, ('row', 'col')), may hold values from -0.046875 to 0.046875
- a_cols: int32 [16, 2, 64, 8], P('layer', None, ('row', 'col')), may hold values from 0 to 7
- p_blocks: bfloat16 [16, 2, 8, 8, 64, 256], P('layer', None, 'col', 'row'), may hold values from -12 to 12
- p_cols: int32 [16, 2, 8, 8, 4], P('layer', None, 'col', 'row'), may hold values from 0 to 15, as said below
- c_cols: int32 [8, 64, 8], P('col', 'row'), may hold values from 0 to 15, as said below
Outputs:
- c_blocks: bfloat16 [8, 64, 64, 512], P('col', ('row', 'layer'))
The draws below stay inside these ranges and needn't reach their ends.
Inputs may be any that keep to these rules, and one draw needn't show every extreme that they name: `p_cols`: the 4 entries of a block row of P in one column group are distinct. `c_cols`: the 8 entries of a block row of C in one column group are distinct.
All inputs are finite; a program needn't handle non-finite values.
Results may differ from the reference program's by a relative error of at most 0.008.
Values may be sent and summed in bfloat16 or wider, within the bound.
No kernel may reach another device: no remote copies, remote signals or barrier semaphores. Data moves between devices by JAX's collectives and lax.ppermute only.
A program may use at most 64 MiB of HBM per device.

```python
import jax
import jax.numpy as jnp
from jax import lax

BLK = 64
KS = 8
KP = 4
KC = 8
NCC = 16
SECTIONS = 2
LAYERS = 16
GROUPS = 8
RB_ALL = 64
IBS = 8


def pick_distinct(key, leading, width, wanted):
    scores = jax.random.randint(key, leading + (width,), 0, 4096) * width + jnp.arange(width, dtype=jnp.int32)
    order = jnp.argsort(scores, axis=-1)
    return order[..., :wanted].astype(jnp.int32)


def draw_p_cols(key, part):
    return pick_distinct(jax.random.fold_in(key, 11), (LAYERS, SECTIONS, GROUPS, IBS), NCC, KP)


def draw_c_cols(key, part):
    return pick_distinct(jax.random.fold_in(key, 23), (GROUPS, RB_ALL), NCC, KC)


def set_ends(values, own_key, least, largest):
    spot = [jax.random.randint(jax.random.fold_in(own_key, axis), (), 0, length) for axis, length in enumerate(values.shape)]
    widest = values.shape.index(max(values.shape))
    next_to = spot[:widest] + [(spot[widest] + 1) % values.shape[widest]] + spot[widest + 1:]
    return values.at[tuple(spot)].set(least).at[tuple(next_to)].set(largest)


def steps_of(own_key, dims, cuts, low, top_value):
    gain = 1.0
    for position, shards_of in cuts:
        draws = jax.random.uniform(jax.random.fold_in(jax.random.fold_in(own_key, 6), position), (shards_of,), jnp.float32, low / len(cuts), top_value / len(cuts))
        gain = gain * jnp.repeat(jnp.exp(draws), dims[position] // shards_of).reshape((-1,) + (1,) * (len(dims) - 1 - position))
    return gain


def noise(stream_key, extent, spread, most, shards=(), kind=jnp.bfloat16):
    array = jax.random.normal(stream_key, extent, jnp.float32) * spread
    if len(shards) > 0:
        array = steps_of(stream_key, extent, shards, -0.22, 0.18) * array
    return jnp.clip(array, min=-most, max=most).astype(kind)


def setup_inputs(seed: int = 0) -> dict:
    streams_of = jax.random.split(jax.random.key(seed), 6)
    return {
        "a_blocks": noise(streams_of[0], (LAYERS, SECTIONS, RB_ALL, BLK, KS * BLK), (BLK * KS * SECTIONS * LAYERS) ** -0.5, 0.046875, ((0, 16), (2, 32))),
        "a_cols": set_ends(jax.random.randint(streams_of[1], (LAYERS, SECTIONS, RB_ALL, KS), 0, IBS), jax.random.fold_in(streams_of[1], 1), 0, IBS - 1).astype(jnp.int32),
        "p_blocks": noise(streams_of[2], (LAYERS, SECTIONS, GROUPS, IBS, BLK, KP * BLK), 2.0, 12.0, ((0, 16), (2, 8), (3, 4))),
        "p_cols": draw_p_cols(jax.random.fold_in(streams_of[5], 71), 0),
        "c_cols": draw_c_cols(jax.random.fold_in(streams_of[5], 71), 0),
    }


def reference(a_blocks, a_cols, p_blocks, p_cols, c_cols):
    a_flat = a_blocks.reshape(LAYERS * SECTIONS, RB_ALL, BLK, KS * BLK)
    idx_flat = a_cols.reshape(LAYERS * SECTIONS, RB_ALL, KS)

    def one_group(inputs):
        p_group, pc_group, targets = inputs
        p_flat = p_group.reshape(LAYERS * SECTIONS, IBS, BLK, KP * BLK)
        pc_flat = pc_group.reshape(LAYERS * SECTIONS, IBS, KP)

        def advance(running, pieces):
            a_strip, row_idx, p_panel, panel_idx = pieces
            picked = p_panel[row_idx].astype(jnp.float32)
            a_four = a_strip.astype(jnp.float32).reshape(RB_ALL, BLK, KS, BLK)
            prods = jnp.einsum('ixky,ikyz->ikxz', a_four, picked).reshape(RB_ALL, KS, BLK, KP, BLK)
            coarse = panel_idx[row_idx]
            onehot = (coarse[:, :, :, None] == targets[:, None, None, :]).astype(jnp.float32)
            placed = jnp.einsum('ikxjz,ikjm->ixmz', prods, onehot).reshape(RB_ALL, BLK, KC * BLK)
            return running + placed, None

        start_acc = jnp.zeros((RB_ALL, BLK, KC * BLK), jnp.float32)
        summed, _ = lax.scan(advance, start_acc, (a_flat, idx_flat, p_flat, pc_flat))
        return summed.astype(jnp.bfloat16)

    return lax.map(one_group, (jnp.moveaxis(p_blocks, 2, 0), jnp.moveaxis(p_cols, 2, 0), c_cols))
```

```python
import jax
import jax.numpy as jnp
from jax import lax
from jax.experimental import pallas as pl
from jax.experimental.pallas import tpu as pltpu
from jax.sharding import PartitionSpec as P


BLK = 64
KS = 8
KP = 4
KC = 8
NCC = 16
SEC = 2
OWN = 2
HEAD = 16
BODY = SEC * OWN * BLK
PAIR = 2 * BLK


def pack(blocks, cols, width):
    body = blocks.reshape(BODY, width)
    head = jnp.pad(cols.reshape(-1).astype(jnp.bfloat16), (0, HEAD * width - cols.size))
    return jnp.concatenate([body, head.reshape(HEAD, width)], axis=0)


def twins(two):
    turned = pltpu.roll(two, BLK, 1)
    low = lax.broadcasted_iota(jnp.int32, two.shape, 1) < BLK
    return jnp.where(low, two, turned), jnp.where(low, turned, two)


def kernel(num_rows, num_cols, sub, idx, *refs):
    own_a = refs[:4]
    other_a = refs[4]
    p_parts = refs[5:9]
    out, wide, full = refs[9:]
    my_row, my_col = idx[0], idx[1]
    p_at, a_at, c_at = 2, 2 + 64, 2 + 64 + 256
    half = lax.broadcasted_iota(jnp.int32, (BLK, PAIR), 1) // BLK

    for d in range(4):
        src = lax.rem(my_row - d + num_rows, num_rows)

        def spread(n, _, d=d, src=src):
            s, j = n // OWN, lax.rem(n, OWN)
            first = pl.multiple_of(n * BLK, BLK)
            copies = []
            for pair in range(KP // 2):
                two = p_parts[d][pl.ds(first, BLK), pair * PAIR : (pair + 1) * PAIR]
                copies.extend(twins(two.astype(jnp.float32)))
            slab = pl.multiple_of((s * 8 + src * OWN + j) * BLK, BLK)
            cols = [idx[p_at + (d * SEC * OWN + n) * KP + q] for q in range(KP)]
            for pair in range(NCC // 2):
                acc = jnp.zeros((BLK, PAIR), jnp.float32)
                for q in range(KP):
                    acc = jnp.where(half + 2 * pair == cols[q], copies[q], acc)
                wide[pl.ds(slab, BLK), pair * PAIR : (pair + 1) * PAIR] = acc.astype(jnp.bfloat16)
            return 0

        lax.fori_loop(0, SEC * OWN, spread, 0)

    def one_row(ref, base, slot, src, j):
        i = src * OWN + j
        left, right = [], []
        for s in range(SEC):
            first = pl.multiple_of(base + (s * OWN + j) * BLK, BLK)
            left.append(ref[pl.ds(first, BLK), :])
            for k in range(KS):
                b = idx[a_at + ((slot * SEC + s) * OWN + j) * KS + k]
                right.append(wide[pl.ds(pl.multiple_of((s * 8 + b) * BLK, BLK), BLK), :])
        full[...] = jnp.dot(
            jnp.concatenate(left, axis=1), jnp.concatenate(right, axis=0), preferred_element_type=jnp.float32
        )
        for pair in range(KC // 2):
            picked = []
            for m in range(2):
                c = idx[c_at + i * KC + pair * 2 + m]
                two = full[:, pl.ds(pl.multiple_of((c // 2) * PAIR, PAIR), PAIR)]
                picked.append(jnp.where(half * 0 + lax.rem(c, 2) == m, two, pltpu.roll(two, BLK, 1)))
            out[lax.rem(i, sub), i // sub, :, pair * PAIR : (pair + 1) * PAIR] = jnp.where(
                half == 0, picked[0], picked[1]
            ).astype(jnp.bfloat16)

    for d in range(4):
        src = lax.rem(my_col - 2 * d + num_cols, num_cols)

        def body(j, _, d=d, src=src):
            one_row(own_a[d], 0, d, src, j)
            return 0

        lax.fori_loop(0, OWN, body, 0)

    def other(n, _):
        d, j = n // OWN, lax.rem(n, OWN)
        src = lax.rem(my_col + 1 - 2 * lax.rem(my_col, 2) - 2 * d + num_cols, num_cols)
        one_row(other_a, d * (BODY + HEAD), 4 + d, src, j)
        return 0

    lax.fori_loop(0, 4 * OWN, other, 0)


def local(a_blocks, a_cols, p_blocks, p_cols, c_cols):
    rows, cols, layers = lax.axis_size("row"), lax.axis_size("col"), lax.axis_size("layer")
    sub = 4
    a_own = pack(a_blocks, a_cols, KS * BLK)
    p_own = pack(p_blocks, p_cols, KP * BLK)
    a_parts = [a_own] + [
        lax.ppermute(a_own, "col", [(i, (i + 2 * d) % cols) for i in range(cols)]) for d in range(1, cols // 2)
    ]
    p_parts = [p_own] + [lax.ppermute(p_own, "row", [(i, (i + d) % rows) for i in range(rows)]) for d in range(1, rows)]
    a_other = lax.ppermute(jnp.concatenate(a_parts, axis=0), "col", [(i, i ^ 1) for i in range(cols)])
    a_idx = [p[BODY, : SEC * OWN * KS] for p in a_parts]
    a_idx += [a_other[d * (BODY + HEAD) + BODY, : SEC * OWN * KS] for d in range(cols // 2)]
    p_idx = [p[BODY, : SEC * OWN * KP] for p in p_parts]
    idx = jnp.concatenate(
        [jnp.stack([lax.axis_index("row"), lax.axis_index("col")]).astype(jnp.int32)]
        + [v.astype(jnp.int32) for v in p_idx + a_idx]
        + [c_cols.reshape(-1)]
    )
    block = (BLK, KC * BLK)
    partial = pl.pallas_call(
        lambda *refs: kernel(rows, cols, sub, *refs),
        out_shape=jax.ShapeDtypeStruct((sub, layers // sub) + block, jnp.bfloat16),
        in_specs=[pl.BlockSpec(memory_space=pltpu.SMEM)] + [pl.BlockSpec(memory_space=pltpu.VMEM)] * 9,
        out_specs=pl.BlockSpec(memory_space=pltpu.VMEM),
        scratch_shapes=[
            pltpu.VMEM((SEC * 8 * BLK, NCC * BLK), jnp.bfloat16),
            pltpu.VMEM((BLK, NCC * BLK), jnp.float32),
        ],
        cost_estimate=pl.CostEstimate(flops=2 * 10**9, bytes_accessed=4 * 10**6, transcendentals=0),
        compiler_params=pltpu.CompilerParams(vmem_limit_bytes=32 * 1024 * 1024),
    )(idx, *a_parts, a_other, *p_parts)
    near = [[g * sub + i for i in range(sub)] for g in range(layers // sub)]
    far = [[g + i * sub for i in range(layers // sub)] for g in range(sub)]
    got = lax.all_to_all(partial, "layer", 0, 0, axis_index_groups=near, tiled=True)
    part = got.astype(jnp.float32).sum(axis=0).astype(jnp.bfloat16)
    got = lax.all_to_all(part, "layer", 0, 0, axis_index_groups=far, tiled=True)
    return got.astype(jnp.float32).sum(axis=0).astype(jnp.bfloat16)[None, None]


def solution(mesh):
    return jax.shard_map(
        local,
        mesh=mesh,
        in_specs=(
            P("layer", None, ("row", "col"), None, None),
            P("layer", None, ("row", "col"), None),
            P("layer", None, "col", "row", None, None),
            P("layer", None, "col", "row", None),
            P("col", "row", None),
        ),
        out_specs=P("col", ("row", "layer"), None, None),
        check_vma=False,
    )
```

```python
import jax
import jax.numpy as jnp
from jax import lax
from jax.experimental import pallas as pl
from jax.experimental.pallas import tpu as pltpu
from jax.sharding import PartitionSpec as P


BLK = 64
KS = 8
KP = 4
KC = 8
NCC = 16
SEC = 2
OWN = 2
IBS = 8
CORES = 2
HEAD = 16
BODY = SEC * OWN * BLK
PAIR = 2 * BLK
STEP = 16
P_AT = 1
A_AT = P_AT + SEC * IBS * KP
VMEM = pl.BlockSpec(memory_space=pltpu.VMEM)
SMEM = pl.BlockSpec(memory_space=pltpu.SMEM)


def repeat(count, unroll, step):
    def several(t, _):
        for u in range(unroll):
            step(t * unroll + u)
        return 0

    lax.fori_loop(0, count // unroll, several, 0)


def head_row(cols, count, width):
    lane = lax.broadcasted_iota(jnp.int32, (HEAD, width), 1)
    row = jnp.zeros((HEAD, width), jnp.float32)
    for n in range(count):
        row = jnp.where(lane == n, cols[n].astype(jnp.float32), row)
    return row.astype(jnp.bfloat16)


def pack_kernel(a_cols, p_cols, a_blocks, p_blocks, a_out, p_out):
    a_head = head_row(a_cols, SEC * OWN * KS, PAIR)
    p_head = head_row(p_cols, SEC * OWN * KP, PAIR)
    for n in range(a_out.shape[0]):
        a_out[n, :BODY, :] = a_blocks[...]
        a_out[n, BODY:, :] = jnp.zeros((HEAD, KS * BLK), jnp.bfloat16)
        a_out[n, BODY:, :PAIR] = a_head
    for n in range(p_out.shape[0]):
        p_out[n, :BODY, :] = p_blocks[...]
        p_out[n, BODY:, :] = jnp.zeros((HEAD, KP * BLK), jnp.bfloat16)
        p_out[n, BODY:, :PAIR] = p_head


def twins(two):
    turned = pltpu.roll(two, BLK, 1)
    low = lax.broadcasted_iota(jnp.int32, two.shape, 1) < BLK
    return jnp.where(low, two, turned), jnp.where(low, turned, two)


def copies_of(tile):
    found = []
    for t in range(tile.shape[1] // PAIR):
        found.extend(twins(tile[:, t * PAIR : (t + 1) * PAIR].astype(jnp.float32)))
    return found


def product_kernel(near, idx, a_ref, b_ref, p_ref, out, wide, rows, full):
    core = idx[0]
    parts = a_ref.shape[0]
    c_at = A_AT + CORES * parts * SEC * OWN * KS
    half = lax.broadcasted_iota(jnp.int32, (STEP, PAIR), 1) // BLK

    def spread(n):
        src, s, j = n // (SEC * OWN), lax.rem(n // OWN, SEC), lax.rem(n, OWN)
        cols = [idx[P_AT + n * KP + q] for q in range(KP)]
        slab = pl.multiple_of((s * IBS + src * OWN + j) * BLK, BLK)
        for g in range(BLK // STEP):
            first = pl.multiple_of((s * OWN + j) * BLK + g * STEP, STEP)
            copies = copies_of(p_ref[src, pl.ds(first, STEP), :])
            for pair in range(NCC // 2):
                acc = jnp.where(half == cols[0] - 2 * pair, copies[0], 0.0)
                for q in range(1, KP):
                    acc = jnp.where(half == cols[q] - 2 * pair, copies[q], acc)
                wide[pl.ds(slab + g * STEP, STEP), pair * PAIR : (pair + 1) * PAIR] = acc.astype(jnp.bfloat16)

    repeat(p_ref.shape[0] * SEC * OWN, 4, spread)

    for side, ref in enumerate((a_ref, b_ref)):

        def gather(n, side=side, ref=ref):
            src, j = n // OWN, lax.rem(n, OWN)
            row = pl.multiple_of((side * parts * OWN + n) * BLK, BLK)
            for s in range(SEC):
                at = A_AT + (((side * parts + src) * SEC + s) * OWN + j) * KS
                cols = [idx[at + k] for k in range(KS)]
                for g in range(BLK // STEP):
                    first = pl.multiple_of((s * OWN + j) * BLK + g * STEP, STEP)
                    copies = copies_of(ref[src, pl.ds(first, STEP), :])
                    for pair in range(IBS // 2):
                        acc = jnp.where(half == cols[0] - 2 * pair, copies[0], 0.0)
                        for k in range(1, KS):
                            acc = acc + jnp.where(half == cols[k] - 2 * pair, copies[k], 0.0)
                        lanes = slice((s * IBS // 2 + pair) * PAIR, (s * IBS // 2 + pair + 1) * PAIR)
                        rows[pl.ds(row + g * STEP, STEP), lanes] = acc.astype(jnp.bfloat16)

        repeat(parts * OWN, 4, gather)

    full[...] = jnp.dot(rows[...], wide[...], preferred_element_type=jnp.float32)
    low = lax.broadcasted_iota(jnp.int32, (BLK, PAIR), 1) < BLK

    for side in range(CORES):
        other = core if side == 0 else 1 - core

        def pick(n, side=side, other=other):
            i = (n // OWN * CORES + other) * OWN + lax.rem(n, OWN)
            row = pl.multiple_of((side * parts * OWN + n) * BLK, BLK)
            for pair in range(KC // 2):
                picked = []
                for m in range(2):
                    c = idx[c_at + i * KC + pair * 2 + m]
                    two = full[pl.ds(row, BLK), pl.ds(pl.multiple_of(c // 2 * PAIR, PAIR), PAIR)]
                    picked.append(jnp.where(lax.rem(c, 2) == m, two, pltpu.roll(two, BLK, 1)))
                out[lax.rem(i, near), i // near, :, pair * PAIR : (pair + 1) * PAIR] = jnp.where(
                    low, picked[0], picked[1]
                ).astype(jnp.bfloat16)

        repeat(parts * OWN, 8, pick)


def local(a_blocks, a_cols, p_blocks, p_cols, c_cols):
    rows, cols, layers = lax.axis_size("row"), lax.axis_size("col"), lax.axis_size("layer")
    chips = cols // CORES
    near = 4
    a_out, p_out = pl.pallas_call(
        pack_kernel,
        out_shape=(
            jax.ShapeDtypeStruct((chips, BODY + HEAD, KS * BLK), jnp.bfloat16),
            jax.ShapeDtypeStruct((rows, BODY + HEAD, KP * BLK), jnp.bfloat16),
        ),
        in_specs=[SMEM, SMEM, VMEM, VMEM],
        out_specs=(VMEM, VMEM),
    )(
        a_cols.reshape(-1),
        p_cols.reshape(-1),
        a_blocks.reshape(BODY, KS * BLK),
        p_blocks.reshape(BODY, KP * BLK),
    )
    same_core = [[chip * CORES + core for chip in range(chips)] for core in range(CORES)]
    a_own = lax.all_to_all(a_out, "col", 0, 0, axis_index_groups=same_core, tiled=True)
    p_all = lax.all_to_all(p_out, "row", 0, 0, tiled=True)
    a_other = lax.ppermute(a_own, "col", [(i, i ^ 1) for i in range(cols)])
    idx = jnp.concatenate(
        [
            v.astype(jnp.int32).reshape(-1)
            for v in (
                lax.rem(lax.axis_index("col"), CORES),
                p_all[:, BODY, : SEC * OWN * KP],
                a_own[:, BODY, : SEC * OWN * KS],
                a_other[:, BODY, : SEC * OWN * KS],
                c_cols,
            )
        ]
    )
    partial = pl.pallas_call(
        lambda *refs: product_kernel(near, *refs),
        out_shape=jax.ShapeDtypeStruct((near, layers // near, BLK, KC * BLK), jnp.bfloat16),
        in_specs=[SMEM, VMEM, VMEM, VMEM],
        out_specs=VMEM,
        scratch_shapes=[
            pltpu.VMEM((SEC * IBS * BLK, NCC * BLK), jnp.bfloat16),
            pltpu.VMEM((cols * OWN * BLK, SEC * IBS * BLK), jnp.bfloat16),
            pltpu.VMEM((cols * OWN * BLK, NCC * BLK), jnp.float32),
        ],
        cost_estimate=pl.CostEstimate(flops=2 * 10**9, bytes_accessed=4 * 10**6, transcendentals=0),
        compiler_params=pltpu.CompilerParams(vmem_limit_bytes=32 * 1024 * 1024),
    )(idx, a_own, a_other, p_all)

    def group(col, g):
        first = near * g + (near // 2) * (col % CORES)
        found = sorted(range(first, first + near), key=lambda z: z % near)
        return [col * layers + z % layers for z in found]

    close = [group(col, g) for col in range(cols) for g in range(layers // near)]
    far = [[o + near * g for g in range(layers // near)] for o in range(near)]
    got = lax.all_to_all(partial, ("col", "layer"), 0, 0, axis_index_groups=close, tiled=True)
    part = got.astype(jnp.float32).sum(axis=0).astype(jnp.bfloat16)
    got = lax.all_to_all(part, "layer", 0, 0, axis_index_groups=far, tiled=True)
    return got.astype(jnp.float32).sum(axis=0).astype(jnp.bfloat16)[None, None]


def solution(mesh):
    return jax.shard_map(
        local,
        mesh=mesh,
        in_specs=(
            P("layer", None, ("row", "col"), None, None),
            P("layer", None, ("row", "col"), None),
            P("layer", None, "col", "row", None, None),
            P("layer", None, "col", "row", None),
            P("col", "row", None),
        ),
        out_specs=P("col", ("row", "layer"), None, None),
        check_vma=False,
    )
```

```python
import jax
import jax.numpy as jnp
from jax import lax
from jax.experimental import pallas as pl
from jax.experimental.pallas import tpu as pltpu
from jax.sharding import PartitionSpec as P


BLK = 64
KS = 8
KP = 4
KC = 8
NCC = 16
SEC = 2
OWN = 2
IBS = 8
CORES = 2
HEAD = 16
BODY = SEC * OWN * BLK
PAIR = 2 * BLK
SMALL = 8 * 1024 * 1024
STEP = 16
VMEM = pl.BlockSpec(memory_space=pltpu.VMEM)
SMEM = pl.BlockSpec(memory_space=pltpu.SMEM)


def repeat(count, unroll, step):
    def several(t, _):
        for u in range(unroll):
            step(t * unroll + u)
        return 0

    lax.fori_loop(0, count // unroll, several, 0)


def head_row(values):
    lane = lax.broadcasted_iota(jnp.int32, (HEAD, PAIR), 1)
    row = jnp.zeros((HEAD, PAIR), jnp.float32)
    for n, value in enumerate(values):
        row = jnp.where(lane == n, value.astype(jnp.float32), row)
    return row.astype(jnp.bfloat16)


def pack_kernel(a_cols, p_cols, a_blocks, p_blocks, a_out, p_out):
    a_head = head_row([a_cols[0, s, j, k] for s in range(SEC) for j in range(OWN) for k in range(KS)])
    p_head = head_row([p_cols[0, s, 0, j, q] for s in range(SEC) for j in range(OWN) for q in range(KP)])
    for n in range(a_out.shape[0]):
        a_out[n, :BODY, :] = a_blocks[...]
        a_out[n, BODY:, :] = jnp.zeros((HEAD, KS * BLK), jnp.bfloat16)
        a_out[n, BODY:, :PAIR] = a_head
    p_out[:BODY, :] = p_blocks[...]
    p_out[BODY:, :] = jnp.zeros((HEAD, KP * BLK), jnp.bfloat16)
    p_out[BODY:, :PAIR] = p_head


def twins(two):
    turned = pltpu.roll(two, BLK, 1)
    low = lax.broadcasted_iota(jnp.int32, two.shape, 1) < BLK
    return jnp.where(low, two, turned), jnp.where(low, turned, two)


def copies_of(tile):
    found = []
    for t in range(tile.shape[1] // PAIR):
        found.extend(twins(tile[:, t * PAIR : (t + 1) * PAIR].astype(jnp.float32)))
    return found


def swap(tile):
    return jnp.concatenate([tile[:, BLK:], tile[:, :BLK]], axis=1)


def masks_of(head, first, count, pairs):
    place = (lax.broadcasted_iota(jnp.int32, (STEP, PAIR), 1) // BLK).astype(jnp.float32)
    cols = [jnp.broadcast_to(head[:, first + n : first + n + 1], (STEP, PAIR)) for n in range(count)]
    return [[place + 2 * pair == col for col in cols] for pair in range(pairs)]


def expand_kernel(own, *refs):
    p_parts, wide = refs[:-1], refs[-1]
    for d, p_ref in enumerate(p_parts):
        src = lax.rem(own[1] - d + len(p_parts), len(p_parts))
        head = p_ref[BODY:, :PAIR].astype(jnp.float32)
        for n in range(SEC * OWN):
            s, j = n // OWN, n % OWN
            masks = masks_of(head, n * KP, KP, NCC // 2)
            slab = pl.multiple_of((s * IBS + src * OWN + j) * BLK, BLK)
            for g in range(BLK // STEP):
                copies = copies_of(p_ref[n * BLK + g * STEP : n * BLK + (g + 1) * STEP, :])
                for pair in range(NCC // 2):
                    acc = jnp.where(masks[pair][0], copies[0], 0.0)
                    for q in range(1, KP):
                        acc = jnp.where(masks[pair][q], copies[q], acc)
                    wide[pl.ds(slab + g * STEP, STEP), pair * PAIR : (pair + 1) * PAIR] = acc.astype(jnp.bfloat16)


def product_kernel(near, side, own, a_ref, wide, *refs):
    out, rows, full = refs[-3:]
    owner = own[0] if side == 0 else 1 - own[0]
    parts = a_ref.shape[0]
    c_at = 2

    def gather(src):
        head = a_ref[src, BODY:, :PAIR].astype(jnp.float32)
        for j in range(OWN):
            row = pl.multiple_of((src * OWN + j) * BLK, BLK)
            for s in range(SEC):
                masks = masks_of(head, (s * OWN + j) * KS, KS, IBS // 2)
                for g in range(BLK // STEP):
                    first = (s * OWN + j) * BLK + g * STEP
                    copies = copies_of(a_ref[src, first : first + STEP, :])
                    for pair in range(IBS // 2):
                        acc = jnp.where(masks[pair][0], copies[0], 0.0)
                        for k in range(1, KS):
                            acc = acc + jnp.where(masks[pair][k], copies[k], 0.0)
                        lanes = slice((s * IBS // 2 + pair) * PAIR, (s * IBS // 2 + pair + 1) * PAIR)
                        rows[pl.ds(row + g * STEP, STEP), lanes] = acc.astype(jnp.bfloat16)

    repeat(parts, 2, gather)
    full[...] = jnp.dot(rows[...], wide[...], preferred_element_type=jnp.float32).astype(jnp.bfloat16)
    low = lax.broadcasted_iota(jnp.int32, (BLK, PAIR), 1).astype(jnp.int16) < jnp.int16(BLK)

    def pick(n):
        i = (n // OWN * CORES + owner) * OWN + lax.rem(n, OWN)
        row = pl.multiple_of(n * BLK, BLK)
        for pair in range(KC // 2):
            picked = []
            for m in range(2):
                c = own[c_at + i * KC + pair * 2 + m]
                two = full[pl.ds(row, BLK), pl.ds(pl.multiple_of(c // 2 * PAIR, PAIR), PAIR)]
                picked.append(jnp.where(lax.rem(c, 2) == m, two, swap(two)))
            out[lax.rem(i, near), i // near, :, pair * PAIR : (pair + 1) * PAIR] = jnp.where(low, *picked)

    repeat(parts * OWN, 8, pick)


def local(a_blocks, a_cols, p_blocks, p_cols, c_cols):
    rows, chips, layers = lax.axis_size("row"), lax.axis_size("chip"), lax.axis_size("layer")
    near = 4
    a_out, p_out = pl.pallas_call(
        pack_kernel,
        out_shape=(
            jax.ShapeDtypeStruct((chips, BODY + HEAD, KS * BLK), jnp.bfloat16),
            jax.ShapeDtypeStruct((BODY + HEAD, KP * BLK), jnp.bfloat16),
        ),
        in_specs=[SMEM, SMEM, VMEM, VMEM],
        out_specs=(VMEM, VMEM),
    )(a_cols, p_cols, a_blocks.reshape(BODY, KS * BLK), p_blocks.reshape(BODY, KP * BLK))
    a_own = lax.all_to_all(a_out, "chip", 0, 0, tiled=True)
    p_parts = [p_out] + [lax.ppermute(p_out, "row", [(i, (i + d) % rows) for i in range(rows)]) for d in range(1, rows)]
    a_other = lax.ppermute(a_own, "core", [(0, 1), (1, 0)])
    own = jnp.stack([lax.axis_index("core"), lax.axis_index("row")]).astype(jnp.int32)
    own = jnp.concatenate([own, c_cols.reshape(-1)])
    wide = pl.pallas_call(
        expand_kernel,
        out_shape=jax.ShapeDtypeStruct((SEC * IBS * BLK, NCC * BLK), jnp.bfloat16),
        in_specs=[SMEM] + [VMEM] * rows,
        out_specs=VMEM,
        cost_estimate=pl.CostEstimate(flops=10**6, bytes_accessed=3 * 10**6, transcendentals=0),
        compiler_params=pltpu.CompilerParams(vmem_limit_bytes=SMALL),
    )(own, *p_parts)

    def products(side, part_of_a, *so_far):
        return pl.pallas_call(
            lambda *refs: product_kernel(near, side, *refs),
            out_shape=jax.ShapeDtypeStruct((near, layers // near, BLK, KC * BLK), jnp.bfloat16),
            in_specs=[SMEM] + [VMEM] * 2 + [pl.BlockSpec(memory_space=pl.ANY)] * len(so_far),
            out_specs=VMEM,
            scratch_shapes=[
                pltpu.VMEM((chips * OWN * BLK, SEC * IBS * BLK), jnp.bfloat16),
                pltpu.VMEM((chips * OWN * BLK, NCC * BLK), jnp.bfloat16),
            ],
            input_output_aliases={3: 0} if so_far else {},
            cost_estimate=pl.CostEstimate(flops=10**9, bytes_accessed=4 * 10**6, transcendentals=0),
            compiler_params=pltpu.CompilerParams(vmem_limit_bytes=2 * SMALL),
        )(own, part_of_a, wide, *so_far)

    partial = products(1, a_other, products(0, a_own))

    def group(core, g):
        first = near * g + (near // 2) * core
        found = sorted(range(first, first + near), key=lambda z: z % near)
        return [core * layers + z % layers for z in found]

    close = [group(core, g) for core in range(CORES) for g in range(layers // near)]
    far = [[o + near * g for g in range(layers // near)] for o in range(near)]
    got = lax.all_to_all(partial, ("core", "layer"), 0, 0, axis_index_groups=close, tiled=True)
    part = got.astype(jnp.float32).sum(axis=0).astype(jnp.bfloat16)
    got = lax.all_to_all(part, "layer", 0, 0, axis_index_groups=far, tiled=True)
    return got.astype(jnp.float32).sum(axis=0).astype(jnp.bfloat16)[None, None]


def solution(mesh):
    rows, cols, layers = mesh.devices.shape
    split = jax.sharding.Mesh(
        mesh.devices.reshape(rows, cols // CORES, CORES, layers), ("row", "chip", "core", "layer")
    )
    col = ("chip", "core")
    return jax.shard_map(
        local,
        mesh=split,
        in_specs=(
            P("layer", None, ("row",) + col, None, None),
            P("layer", None, ("row",) + col, None),
            P("layer", None, col, "row", None, None),
            P("layer", None, col, "row", None),
            P(col, "row", None),
        ),
        out_specs=P(col, ("row", "layer"), None, None),
        check_vma=False,
    )
```

```python
import jax
import jax.numpy as jnp
from jax import lax
from jax.experimental import pallas as pl
from jax.experimental.pallas import tpu as pltpu
from jax.sharding import PartitionSpec as P


BLK = 64
KS = 8
KP = 4
KC = 8
NCC = 16
SEC = 2
OWN = 2
IBS = 8
CORES = 2
HEAD = 16
BODY = SEC * OWN * BLK
PAIR = 2 * BLK
SMALL = 8 * 1024 * 1024
STEP = 16
VMEM = pl.BlockSpec(memory_space=pltpu.VMEM)
SMEM = pl.BlockSpec(memory_space=pltpu.SMEM)
HBM = pl.BlockSpec(memory_space=pltpu.HBM)


def repeat(count, unroll, step):
    def several(t, _):
        for u in range(unroll):
            step(t * unroll + u)
        return 0

    lax.fori_loop(0, count // unroll, several, 0)


def head_row(values):
    lane = lax.broadcasted_iota(jnp.int32, (HEAD, PAIR), 1)
    row = jnp.zeros((HEAD, PAIR), jnp.float32)
    for n, value in enumerate(values):
        row = jnp.where(lane == n, value.astype(jnp.float32), row)
    return row.astype(jnp.bfloat16)


def pack_kernel(a_cols_hbm, p_cols_hbm, a_blocks, p_blocks, a_out, p_out, a_cols, p_cols, sems):
    places = [a_out.at[n, :BODY] for n in range(a_out.shape[0])]
    moves = [(a_cols_hbm, a_cols), (p_cols_hbm, p_cols), (p_blocks, p_out.at[:BODY])]
    moves += [(a_blocks, place) for place in places]
    copies = [pltpu.make_async_copy(src, dst, sems.at[n]) for n, (src, dst) in enumerate(moves)]
    for copy in copies:
        copy.start()
    copies[0].wait()
    copies[1].wait()
    a_head = head_row([a_cols[0, s, j, k] for s in range(SEC) for j in range(OWN) for k in range(KS)])
    p_head = head_row([p_cols[0, s, 0, j, q] for s in range(SEC) for j in range(OWN) for q in range(KP)])
    for n in range(a_out.shape[0]):
        a_out[n, BODY:, :] = jnp.zeros((HEAD, KS * BLK), jnp.bfloat16)
        a_out[n, BODY:, :PAIR] = a_head
    p_out[BODY:, :] = jnp.zeros((HEAD, KP * BLK), jnp.bfloat16)
    p_out[BODY:, :PAIR] = p_head
    for copy in copies[2:]:
        copy.wait()


def twins(two):
    turned = pltpu.roll(two, BLK, 1)
    low = lax.broadcasted_iota(jnp.int32, two.shape, 1) < BLK
    return jnp.where(low, two, turned), jnp.where(low, turned, two)


def copies_of(tile):
    found = []
    for t in range(tile.shape[1] // PAIR):
        found.extend(twins(tile[:, t * PAIR : (t + 1) * PAIR].astype(jnp.float32)))
    return found


def swap(tile):
    return jnp.concatenate([tile[:, BLK:], tile[:, :BLK]], axis=1)


def masks_of(head, first, count, pairs):
    place = (lax.broadcasted_iota(jnp.int32, (STEP, PAIR), 1) // BLK).astype(jnp.float32)
    cols = [jnp.broadcast_to(head[:, first + n : first + n + 1], (STEP, PAIR)) for n in range(count)]
    return [[place + 2 * pair == col for col in cols] for pair in range(pairs)]


def expand_kernel(*refs):
    held, sems = refs[-2:]
    p_parts, wide = refs[:-3], refs[-3]
    copies = [pltpu.make_async_copy(part, held.at[d], sems.at[d]) for d, part in enumerate(p_parts)]
    for copy in copies:
        copy.start()
    for d, copy in enumerate(copies):
        copy.wait()
        p_ref = held.at[d]
        src = lax.rem(lax.axis_index("row") - d + len(p_parts), len(p_parts))
        head = p_ref[BODY:, :PAIR].astype(jnp.float32)
        for n in range(SEC * OWN):
            s, j = n // OWN, n % OWN
            masks = masks_of(head, n * KP, KP, NCC // 2)
            slab = pl.multiple_of((s * IBS + src * OWN + j) * BLK, BLK)
            for g in range(BLK // STEP):
                copies = copies_of(p_ref[n * BLK + g * STEP : n * BLK + (g + 1) * STEP, :])
                for pair in range(NCC // 2):
                    acc = jnp.where(masks[pair][0], copies[0], 0.0)
                    for q in range(1, KP):
                        acc = jnp.where(masks[pair][q], copies[q], acc)
                    wide[pl.ds(slab + g * STEP, STEP), pair * PAIR : (pair + 1) * PAIR] = acc.astype(jnp.bfloat16)


def product_kernel(near, side, c_cols, a_ref, wide, *refs):
    out, rows, full = refs[-3:]
    core = lax.axis_index("core")
    owner = core if side == 0 else 1 - core
    parts = a_ref.shape[0]

    def gather(src):
        head = a_ref[src, BODY:, :PAIR].astype(jnp.float32)
        for j in range(OWN):
            row = pl.multiple_of((src * OWN + j) * BLK, BLK)
            for s in range(SEC):
                masks = masks_of(head, (s * OWN + j) * KS, KS, IBS // 2)
                for g in range(BLK // STEP):
                    first = (s * OWN + j) * BLK + g * STEP
                    copies = copies_of(a_ref[src, first : first + STEP, :])
                    for pair in range(IBS // 2):
                        acc = jnp.where(masks[pair][0], copies[0], 0.0)
                        for k in range(1, KS):
                            acc = acc + jnp.where(masks[pair][k], copies[k], 0.0)
                        lanes = slice((s * IBS // 2 + pair) * PAIR, (s * IBS // 2 + pair + 1) * PAIR)
                        rows[pl.ds(row + g * STEP, STEP), lanes] = acc.astype(jnp.bfloat16)

    repeat(parts, 2, gather)
    full[...] = jnp.dot(rows[...], wide[...], preferred_element_type=jnp.float32).astype(jnp.bfloat16)
    low = lax.broadcasted_iota(jnp.int32, (BLK, PAIR), 1).astype(jnp.int16) < jnp.int16(BLK)

    def pick(n):
        i = (n // OWN * CORES + owner) * OWN + lax.rem(n, OWN)
        row = pl.multiple_of(n * BLK, BLK)
        for pair in range(KC // 2):
            picked = []
            for m in range(2):
                c = c_cols[0, pair * 2 + m, i]
                two = full[pl.ds(row, BLK), pl.ds(pl.multiple_of(c // 2 * PAIR, PAIR), PAIR)]
                picked.append(jnp.where(lax.rem(c, 2) == m, two, swap(two)))
            out[lax.rem(i, near), i // near, :, pair * PAIR : (pair + 1) * PAIR] = jnp.where(low, *picked)

    repeat(parts * OWN, 8, pick)


def local(a_blocks, a_cols, p_blocks, p_cols, c_cols):
    rows, chips, layers = lax.axis_size("row"), lax.axis_size("chip"), lax.axis_size("layer")
    near = 4
    a_out, p_out = pl.pallas_call(
        pack_kernel,
        out_shape=(
            jax.ShapeDtypeStruct((chips, BODY + HEAD, KS * BLK), jnp.bfloat16),
            jax.ShapeDtypeStruct((BODY + HEAD, KP * BLK), jnp.bfloat16),
        ),
        in_specs=[HBM] * 4,
        out_specs=(VMEM, VMEM),
        scratch_shapes=[
            pltpu.SMEM(a_cols.shape, jnp.int32),
            pltpu.SMEM(p_cols.shape, jnp.int32),
            pltpu.SemaphoreType.DMA((chips + 3,)),
        ],
    )(a_cols, p_cols, a_blocks.reshape(BODY, KS * BLK), p_blocks.reshape(BODY, KP * BLK))
    a_own = lax.all_to_all(a_out, "chip", 0, 0, tiled=True)
    p_parts = [p_out] + [lax.ppermute(p_out, "row", [(i, (i + d) % rows) for i in range(rows)]) for d in range(1, rows)]
    a_other = lax.ppermute(a_own, "core", [(0, 1), (1, 0)])
    wide = pl.pallas_call(
        expand_kernel,
        out_shape=jax.ShapeDtypeStruct((SEC * IBS * BLK, NCC * BLK), jnp.bfloat16),
        in_specs=[HBM] * rows,
        out_specs=VMEM,
        scratch_shapes=[
            pltpu.VMEM((rows, BODY + HEAD, KP * BLK), jnp.bfloat16),
            pltpu.SemaphoreType.DMA((rows,)),
        ],
        cost_estimate=pl.CostEstimate(flops=10**6, bytes_accessed=3 * 10**6, transcendentals=0),
        compiler_params=pltpu.CompilerParams(vmem_limit_bytes=SMALL),
    )(*p_parts)

    def products(side, part_of_a, *so_far):
        return pl.pallas_call(
            lambda *refs: product_kernel(near, side, *refs),
            out_shape=jax.ShapeDtypeStruct((near, layers // near, BLK, KC * BLK), jnp.bfloat16),
            in_specs=[SMEM] + [VMEM] * 2 + [pl.BlockSpec(memory_space=pl.ANY)] * len(so_far),
            out_specs=VMEM,
            scratch_shapes=[
                pltpu.VMEM((chips * OWN * BLK, SEC * IBS * BLK), jnp.bfloat16),
                pltpu.VMEM((chips * OWN * BLK, NCC * BLK), jnp.bfloat16),
            ],
            input_output_aliases={3: 0} if so_far else {},
            cost_estimate=pl.CostEstimate(flops=10**9, bytes_accessed=4 * 10**6, transcendentals=0),
            compiler_params=pltpu.CompilerParams(vmem_limit_bytes=2 * SMALL),
        )(c_cols.transpose(0, 2, 1), part_of_a, wide, *so_far)

    partial = products(1, a_other, products(0, a_own))

    def group(core, g):
        first = near * g + (near // 2) * core
        found = sorted(range(first, first + near), key=lambda z: z % near)
        return [core * layers + z % layers for z in found]

    close = [group(core, g) for core in range(CORES) for g in range(layers // near)]
    far = [[o + near * g for g in range(layers // near)] for o in range(near)]
    got = lax.all_to_all(partial, ("core", "layer"), 0, 0, axis_index_groups=close, tiled=True)
    part = got.astype(jnp.float32).sum(axis=0).astype(jnp.bfloat16)
    got = lax.all_to_all(part, "layer", 0, 0, axis_index_groups=far, tiled=True)
    return got.astype(jnp.float32).sum(axis=0).astype(jnp.bfloat16)[None, None]


def solution(mesh):
    rows, cols, layers = mesh.devices.shape
    split = jax.sharding.Mesh(
        mesh.devices.reshape(rows, cols // CORES, CORES, layers), ("row", "chip", "core", "layer")
    )
    col = ("chip", "core")
    return jax.shard_map(
        local,
        mesh=split,
        in_specs=(
            P("layer", None, ("row",) + col, None, None),
            P("layer", None, ("row",) + col, None),
            P("layer", None, col, "row", None, None),
            P("layer", None, col, "row", None),
            P(col, "row", None),
        ),
        out_specs=P(col, ("row", "layer"), None, None),
        check_vma=False,
    )
```

```python
import jax
import jax.numpy as jnp
from jax import lax
from jax.experimental import pallas as pl
from jax.experimental.pallas import tpu as pltpu
from jax.sharding import PartitionSpec as P


BLK = 64
KS = 8
KP = 4
KC = 8
NCC = 16
SEC = 2
OWN = 2
IBS = 8
CORES = 2
HEAD = 16
BODY = SEC * OWN * BLK
PAIR = 2 * BLK
SMALL = 8 * 1024 * 1024
SHIFTS = ((0, 3), (2, 1))
HALF = 2
STEP = 16
VMEM = pl.BlockSpec(memory_space=pltpu.VMEM)
SMEM = pl.BlockSpec(memory_space=pltpu.SMEM)
HBM = pl.BlockSpec(memory_space=pltpu.HBM)


def repeat(count, unroll, step):
    def several(t, _):
        for u in range(unroll):
            step(t * unroll + u)
        return 0

    lax.fori_loop(0, count // unroll, several, 0)


def head_row(values):
    lane = lax.broadcasted_iota(jnp.int32, (HEAD, PAIR), 1)
    row = jnp.zeros((HEAD, PAIR), jnp.float32)
    for n, value in enumerate(values):
        row = jnp.where(lane == n, value.astype(jnp.float32), row)
    return row.astype(jnp.bfloat16)


def pack_kernel(a_cols, p_cols, a_blocks, p_blocks, a_out, p_out):
    a_head = head_row([a_cols[0, s, j, k] for s in range(SEC) for j in range(OWN) for k in range(KS)])
    p_head = head_row([p_cols[0, s, 0, j, q] for s in range(SEC) for j in range(OWN) for q in range(KP)])
    for n in range(a_out.shape[0]):
        a_out[n, :BODY, :] = a_blocks[...]
        a_out[n, BODY:, :] = jnp.zeros((HEAD, KS * BLK), jnp.bfloat16)
        a_out[n, BODY:, :PAIR] = a_head
    p_out[:BODY, :] = p_blocks[...]
    p_out[BODY:, :] = jnp.zeros((HEAD, KP * BLK), jnp.bfloat16)
    p_out[BODY:, :PAIR] = p_head


def twins(two):
    turned = pltpu.roll(two, BLK, 1)
    low = lax.broadcasted_iota(jnp.int32, two.shape, 1) < BLK
    return jnp.where(low, two, turned), jnp.where(low, turned, two)


def copies_of(tile):
    found = []
    for t in range(tile.shape[1] // PAIR):
        found.extend(twins(tile[:, t * PAIR : (t + 1) * PAIR].astype(jnp.float32)))
    return found


def swap(tile):
    return jnp.concatenate([tile[:, BLK:], tile[:, :BLK]], axis=1)


def masks_of(head, first, count, pairs):
    half = lax.broadcasted_iota(jnp.int32, (STEP, PAIR), 1) // BLK
    cols = [jnp.broadcast_to(head[:, first + n : first + n + 1], (STEP, PAIR)) for n in range(count)]
    return [[(half + 2 * pair).astype(jnp.float32) == col for col in cols] for pair in pairs]


def source_of(shift, axis):
    size = lax.axis_size(axis)
    return lax.rem(lax.axis_index(axis) - shift + size, size)


def expand_kernel(*refs):
    p_parts, (wide, held, sems) = refs[:HALF], refs[HALF:]
    copies = [pltpu.make_async_copy(part, held.at[n], sems.at[n]) for n, part in enumerate(p_parts)]
    for copy in copies:
        copy.start()
    for place, copy in enumerate(copies):
        copy.wait()
        head = held[place, BODY:, :PAIR].astype(jnp.float32)
        for n in range(SEC * OWN):
            s, j = n // OWN, n % OWN
            masks = masks_of(head, n * KP, KP, range(NCC // 2))
            slab = ((s * HALF + place) * OWN + j) * BLK
            for g in range(BLK // STEP):
                copies_in = copies_of(held[place, n * BLK + g * STEP : n * BLK + (g + 1) * STEP, :])
                for pair in range(NCC // 2):
                    acc = jnp.where(masks[pair][0], copies_in[0], 0.0)
                    for q in range(1, KP):
                        acc = jnp.where(masks[pair][q], copies_in[q], acc)
                    first = slab + g * STEP
                    wide[first : first + STEP, pair * PAIR : (pair + 1) * PAIR] = acc.astype(jnp.bfloat16)


def product_kernel(near, c_cols, a_own, a_other, wide_first, wide_second, out, rows, full):
    core = lax.axis_index("core")
    parts = a_own.shape[0]
    sources = [[source_of(shift, "row") for shift in shifts] for shifts in SHIFTS]
    for side, a_ref in enumerate((a_own, a_other)):

        def gather(src, side=side, a_ref=a_ref):
            head = a_ref[src, BODY:, :PAIR].astype(jnp.float32)
            for j in range(OWN):
                row = pl.multiple_of(((side * parts + src) * OWN + j) * BLK, BLK)
                for s in range(SEC):
                    masks = masks_of(head, (s * OWN + j) * KS, KS, sources[0] + sources[1])
                    for g in range(BLK // STEP):
                        first = (s * OWN + j) * BLK + g * STEP
                        copies = copies_of(a_ref[src, first : first + STEP, :])
                        for pair in range(IBS // OWN):
                            acc = jnp.where(masks[pair][0], copies[0], 0.0)
                            for k in range(1, KS):
                                acc = acc + jnp.where(masks[pair][k], copies[k], 0.0)
                            lane = ((pair // HALF * SEC + s) * HALF + pair % HALF) * PAIR
                            rows[pl.ds(row + g * STEP, STEP), lane : lane + PAIR] = acc.astype(jnp.bfloat16)

        repeat(parts, 2, gather)

    wide = jnp.concatenate([wide_first[...], wide_second[...]], axis=0)
    full[...] = jnp.dot(rows[...], wide, preferred_element_type=jnp.float32).astype(jnp.bfloat16)
    low = lax.broadcasted_iota(jnp.int32, (BLK, PAIR), 1).astype(jnp.int16) < jnp.int16(BLK)
    for side in range(CORES):
        owner = core if side == 0 else 1 - core

        def pick(n, side=side, owner=owner):
            i = (n // OWN * CORES + owner) * OWN + lax.rem(n, OWN)
            row = pl.multiple_of((side * parts * OWN + n) * BLK, BLK)
            for pair in range(KC // 2):
                picked = []
                for m in range(2):
                    c = c_cols[0, pair * 2 + m, i]
                    two = full[pl.ds(row, BLK), pl.ds(pl.multiple_of(c // 2 * PAIR, PAIR), PAIR)]
                    picked.append(jnp.where(lax.rem(c, 2) == m, two, swap(two)))
                out[lax.rem(i, near), i // near, :, pair * PAIR : (pair + 1) * PAIR] = jnp.where(low, *picked)

        repeat(parts * OWN, 8, pick)


def local(a_blocks, a_cols, p_blocks, p_cols, c_cols):
    rows, chips, layers = lax.axis_size("row"), lax.axis_size("chip"), lax.axis_size("layer")
    near = 4
    a_out, p_out = pl.pallas_call(
        pack_kernel,
        out_shape=(
            jax.ShapeDtypeStruct((chips, BODY + HEAD, KS * BLK), jnp.bfloat16),
            jax.ShapeDtypeStruct((BODY + HEAD, KP * BLK), jnp.bfloat16),
        ),
        in_specs=[SMEM, SMEM, VMEM, VMEM],
        out_specs=(VMEM, VMEM),
    )(a_cols, p_cols, a_blocks.reshape(BODY, KS * BLK), p_blocks.reshape(BODY, KP * BLK))

    def expand(*parts):
        return pl.pallas_call(
            expand_kernel,
            out_shape=jax.ShapeDtypeStruct((HALF * SEC * OWN * BLK, NCC * BLK), jnp.bfloat16),
            in_specs=[HBM] * HALF,
            out_specs=VMEM,
            scratch_shapes=[
                pltpu.VMEM((HALF, BODY + HEAD, KP * BLK), jnp.bfloat16),
                pltpu.SemaphoreType.DMA((HALF,)),
            ],
            cost_estimate=pl.CostEstimate(flops=10**6, bytes_accessed=2 * 10**6, transcendentals=0),
            compiler_params=pltpu.CompilerParams(vmem_limit_bytes=SMALL),
        )(*parts)

    a_own = lax.all_to_all(a_out, "chip", 0, 0, tiled=True)
    p_parts = [p_out] + [lax.ppermute(p_out, "row", [(i, (i + d) % rows) for i in range(rows)]) for d in range(1, rows)]
    first = expand(*[p_parts[d] for d in SHIFTS[0]])
    a_other = lax.ppermute(a_own, "core", [(0, 1), (1, 0)])
    second = expand(*[p_parts[d] for d in SHIFTS[1]])
    partial = pl.pallas_call(
        lambda *refs: product_kernel(near, *refs),
        out_shape=jax.ShapeDtypeStruct((near, layers // near, BLK, KC * BLK), jnp.bfloat16),
        in_specs=[SMEM] + [VMEM] * 4,
        out_specs=VMEM,
        scratch_shapes=[
            pltpu.VMEM((chips * CORES * OWN * BLK, SEC * IBS * BLK), jnp.bfloat16),
            pltpu.VMEM((chips * CORES * OWN * BLK, NCC * BLK), jnp.bfloat16),
        ],
        cost_estimate=pl.CostEstimate(flops=2 * 10**9, bytes_accessed=4 * 10**6, transcendentals=0),
        compiler_params=pltpu.CompilerParams(vmem_limit_bytes=3 * SMALL),
    )(c_cols.transpose(0, 2, 1), a_own, a_other, first, second)

    def group(core, g):
        first = near * g + (near // 2) * core
        found = sorted(range(first, first + near), key=lambda z: z % near)
        return [core * layers + z % layers for z in found]

    close = [group(core, g) for core in range(CORES) for g in range(layers // near)]
    far = [[o + near * g for g in range(layers // near)] for o in range(near)]
    got = lax.all_to_all(partial, ("core", "layer"), 0, 0, axis_index_groups=close, tiled=True)
    part = got.astype(jnp.float32).sum(axis=0).astype(jnp.bfloat16)
    got = lax.all_to_all(part, "layer", 0, 0, axis_index_groups=far, tiled=True)
    return got.astype(jnp.float32).sum(axis=0).astype(jnp.bfloat16)[None, None]


def solution(mesh):
    rows, cols, layers = mesh.devices.shape
    split = jax.sharding.Mesh(
        mesh.devices.reshape(rows, cols // CORES, CORES, layers), ("row", "chip", "core", "layer")
    )
    col = ("chip", "core")
    return jax.shard_map(
        local,
        mesh=split,
        in_specs=(
            P("layer", None, ("row",) + col, None, None),
            P("layer", None, ("row",) + col, None),
            P("layer", None, col, "row", None, None),
            P("layer", None, col, "row", None),
            P(col, "row", None),
        ),
        out_specs=P(col, ("row", "layer"), None, None),
        check_vma=False,
    )
```

```python
import jax
import jax.numpy as jnp
from jax import lax
from jax.experimental import pallas as pl
from jax.experimental.pallas import tpu as pltpu
from jax.sharding import PartitionSpec as P


BLK = 64
KS = 8
KP = 4
KC = 8
NCC = 16
SEC = 2
OWN = 2
IBS = 8
CORES = 2
HEAD = 16
BODY = SEC * OWN * BLK
PAIR = 2 * BLK
SMALL = 8 * 1024 * 1024
SHIFTS = ((0, 3), (2, 1))
HALF = 2
BATCH = 4
STEP = 16
VMEM = pl.BlockSpec(memory_space=pltpu.VMEM)
SMEM = pl.BlockSpec(memory_space=pltpu.SMEM)
HBM = pl.BlockSpec(memory_space=pltpu.HBM)


def head_row(values):
    lane = lax.broadcasted_iota(jnp.int32, (HEAD, PAIR), 1)
    row = jnp.zeros((HEAD, PAIR), jnp.float32)
    for n, value in enumerate(values):
        row = jnp.where(lane == n, value.astype(jnp.float32), row)
    return row.astype(jnp.bfloat16)


def pack_kernel(a_cols, p_cols, a_blocks, p_blocks, a_out, p_out):
    a_head = head_row([a_cols[0, s, j, k] for s in range(SEC) for j in range(OWN) for k in range(KS)])
    p_head = head_row([p_cols[0, s, 0, j, q] for s in range(SEC) for j in range(OWN) for q in range(KP)])
    for n in range(a_out.shape[0]):
        a_out[n, :BODY, :] = a_blocks[...]
        a_out[n, BODY:, :] = jnp.zeros((HEAD, KS * BLK), jnp.bfloat16)
        a_out[n, BODY:, :PAIR] = a_head
    p_out[:BODY, :] = p_blocks[...]
    p_out[BODY:, :] = jnp.zeros((HEAD, KP * BLK), jnp.bfloat16)
    p_out[BODY:, :PAIR] = p_head


def twins(two):
    turned = pltpu.roll(two, BLK, 1)
    low = lax.broadcasted_iota(jnp.int32, two.shape, 1) < BLK
    return jnp.where(low, two, turned), jnp.where(low, turned, two)


def copies_of(tile):
    found = []
    for t in range(tile.shape[1] // PAIR):
        found.extend(twins(tile[:, t * PAIR : (t + 1) * PAIR].astype(jnp.float32)))
    return found


def swap(tile):
    return jnp.concatenate([tile[:, BLK:], tile[:, :BLK]], axis=1)


def masks_of(head, first, count, pairs):
    half = lax.broadcasted_iota(jnp.int32, (STEP, PAIR), 1) // BLK
    cols = [jnp.broadcast_to(head[:, first + n : first + n + 1], (STEP, PAIR)) for n in range(count)]
    return [[(half + 2 * pair).astype(jnp.float32) == col for col in cols] for pair in pairs]


def source_of(shift, axis):
    size = lax.axis_size(axis)
    return lax.rem(lax.axis_index(axis) - shift + size, size)


def expand_kernel(*refs):
    p_parts, (wide, held, sems) = refs[:HALF], refs[HALF:]
    copies = [pltpu.make_async_copy(part, held.at[n], sems.at[n]) for n, part in enumerate(p_parts)]
    for copy in copies:
        copy.start()
    for place, copy in enumerate(copies):
        copy.wait()
        head = held[place, BODY:, :PAIR].astype(jnp.float32)
        for n in range(SEC * OWN):
            s, j = n // OWN, n % OWN
            masks = masks_of(head, n * KP, KP, range(NCC // 2))
            slab = ((s * HALF + place) * OWN + j) * BLK
            for g in range(BLK // STEP):
                copies_in = copies_of(held[place, n * BLK + g * STEP : n * BLK + (g + 1) * STEP, :])
                for pair in range(NCC // 2):
                    acc = jnp.where(masks[pair][0], copies_in[0], 0.0)
                    for q in range(1, KP):
                        acc = jnp.where(masks[pair][q], copies_in[q], acc)
                    first = slab + g * STEP
                    wide[first : first + STEP, pair * PAIR : (pair + 1) * PAIR] = acc.astype(jnp.bfloat16)


def gather_rows(a_ref, rows):
    sources = [source_of(shift, "row") for shifts in SHIFTS for shift in shifts]
    for src in range(a_ref.shape[0]):
        head = a_ref[src, BODY:, :PAIR].astype(jnp.float32)
        for j in range(OWN):
            row = (src * OWN + j) * BLK
            for s in range(SEC):
                masks = masks_of(head, (s * OWN + j) * KS, KS, sources)
                for g in range(BLK // STEP):
                    first = (s * OWN + j) * BLK + g * STEP
                    copies = copies_of(a_ref[src, first : first + STEP, :])
                    for pair in range(IBS // OWN):
                        acc = jnp.where(masks[pair][0], copies[0], 0.0)
                        for k in range(1, KS):
                            acc = acc + jnp.where(masks[pair][k], copies[k], 0.0)
                        lane = ((pair // HALF * SEC + s) * HALF + pair % HALF) * PAIR
                        rows[row + g * STEP : row + (g + 1) * STEP, lane : lane + PAIR] = acc.astype(jnp.bfloat16)


def product_kernel(near, c_cols, rows_own, a_other, wide_first, wide_second, out, rows_other, *fulls):
    core = lax.axis_index("core")
    block_rows = rows_own.shape[0] // BLK
    low = lax.broadcasted_iota(jnp.int32, (BLK, PAIR), 1).astype(jnp.int16) < jnp.int16(BLK)
    for side, (rows, full) in enumerate(zip((rows_own, rows_other), fulls)):
        owner = core if side == 0 else 1 - core
        if side == 1:
            gather_rows(a_other, rows_other)
        for n in range(block_rows):
            if n % BATCH == 0:
                part = slice(n * BLK, (n + BATCH) * BLK)
                wide = jnp.concatenate([wide_first[...], wide_second[...]], axis=0)
                full[part] = jnp.dot(rows[part], wide, preferred_element_type=jnp.float32).astype(jnp.bfloat16)
            i = (n // OWN * CORES + owner) * OWN + n % OWN
            for pair in range(KC // 2):
                picked = []
                for m in range(2):
                    c = c_cols[0, pair * 2 + m, i]
                    two = full[n * BLK : (n + 1) * BLK, pl.ds(pl.multiple_of(c // 2 * PAIR, PAIR), PAIR)]
                    picked.append(jnp.where(lax.rem(c, 2) == m, two, swap(two)))
                out[lax.rem(i, near), i // near, :, pair * PAIR : (pair + 1) * PAIR] = jnp.where(low, *picked)


def local(a_blocks, a_cols, p_blocks, p_cols, c_cols):
    rows, chips, layers = lax.axis_size("row"), lax.axis_size("chip"), lax.axis_size("layer")
    near = 4
    a_out, p_out = pl.pallas_call(
        pack_kernel,
        out_shape=(
            jax.ShapeDtypeStruct((chips, BODY + HEAD, KS * BLK), jnp.bfloat16),
            jax.ShapeDtypeStruct((BODY + HEAD, KP * BLK), jnp.bfloat16),
        ),
        in_specs=[SMEM, SMEM, VMEM, VMEM],
        out_specs=(VMEM, VMEM),
    )(a_cols, p_cols, a_blocks.reshape(BODY, KS * BLK), p_blocks.reshape(BODY, KP * BLK))

    def expand(*parts):
        return pl.pallas_call(
            expand_kernel,
            out_shape=jax.ShapeDtypeStruct((HALF * SEC * OWN * BLK, NCC * BLK), jnp.bfloat16),
            in_specs=[HBM] * HALF,
            out_specs=VMEM,
            scratch_shapes=[
                pltpu.VMEM((HALF, BODY + HEAD, KP * BLK), jnp.bfloat16),
                pltpu.SemaphoreType.DMA((HALF,)),
            ],
            cost_estimate=pl.CostEstimate(flops=10**6, bytes_accessed=2 * 10**6, transcendentals=0),
            compiler_params=pltpu.CompilerParams(vmem_limit_bytes=SMALL),
        )(*parts)

    a_own = lax.all_to_all(a_out, "chip", 0, 0, tiled=True)
    p_parts = [p_out] + [lax.ppermute(p_out, "row", [(i, (i + d) % rows) for i in range(rows)]) for d in range(1, rows)]
    first = expand(*[p_parts[d] for d in SHIFTS[0]])
    a_other = lax.ppermute(a_own, "core", [(0, 1), (1, 0)])
    rows_own = pl.pallas_call(
        gather_rows,
        out_shape=jax.ShapeDtypeStruct((chips * OWN * BLK, SEC * IBS * BLK), jnp.bfloat16),
        in_specs=[VMEM],
        out_specs=VMEM,
        cost_estimate=pl.CostEstimate(flops=10**6, bytes_accessed=2 * 10**6, transcendentals=0),
        compiler_params=pltpu.CompilerParams(vmem_limit_bytes=SMALL),
    )(a_own)
    second = expand(*[p_parts[d] for d in SHIFTS[1]])
    partial = pl.pallas_call(
        lambda *refs: product_kernel(near, *refs),
        out_shape=jax.ShapeDtypeStruct((near, layers // near, BLK, KC * BLK), jnp.bfloat16),
        in_specs=[SMEM] + [VMEM] * 4,
        out_specs=VMEM,
        scratch_shapes=[
            pltpu.VMEM((chips * OWN * BLK, SEC * IBS * BLK), jnp.bfloat16),
            pltpu.VMEM((chips * OWN * BLK, NCC * BLK), jnp.bfloat16),
            pltpu.VMEM((chips * OWN * BLK, NCC * BLK), jnp.bfloat16),
        ],
        cost_estimate=pl.CostEstimate(flops=2 * 10**9, bytes_accessed=4 * 10**6, transcendentals=0),
        compiler_params=pltpu.CompilerParams(vmem_limit_bytes=3 * SMALL),
    )(c_cols.transpose(0, 2, 1), rows_own, a_other, first, second)

    def group(core, g):
        first = near * g + (near // 2) * core
        found = sorted(range(first, first + near), key=lambda z: z % near)
        return [core * layers + z % layers for z in found]

    close = [group(core, g) for core in range(CORES) for g in range(layers // near)]
    far = [[o + near * g for g in range(layers // near)] for o in range(near)]
    got = lax.all_to_all(partial, ("core", "layer"), 0, 0, axis_index_groups=close, tiled=True)
    part = got.astype(jnp.float32).sum(axis=0).astype(jnp.bfloat16)
    got = lax.all_to_all(part, "layer", 0, 0, axis_index_groups=far, tiled=True)
    return got.astype(jnp.float32).sum(axis=0).astype(jnp.bfloat16)[None, None]


def solution(mesh):
    rows, cols, layers = mesh.devices.shape
    split = jax.sharding.Mesh(
        mesh.devices.reshape(rows, cols // CORES, CORES, layers), ("row", "chip", "core", "layer")
    )
    col = ("chip", "core")
    return jax.shard_map(
        local,
        mesh=split,
        in_specs=(
            P("layer", None, ("row",) + col, None, None),
            P("layer", None, ("row",) + col, None),
            P("layer", None, col, "row", None, None),
            P("layer", None, col, "row", None),
            P(col, "row", None),
        ),
        out_specs=P(col, ("row", "layer"), None, None),
        check_vma=False,
    )
```

```python
import jax
import jax.numpy as jnp
from jax import lax
from jax.experimental import pallas as pl
from jax.experimental.pallas import tpu as pltpu
from jax.sharding import PartitionSpec as P


BLK = 64
KS = 8
KP = 4
KC = 8
NCC = 16
SEC = 2
OWN = 2
IBS = 8
CORES = 2
HEAD = 16
BODY = SEC * OWN * BLK
PAIR = 2 * BLK
SMALL = 8 * 1024 * 1024
SHIFTS = ((0, 3), (2, 1))
HALF = 2
STEP = 16
VMEM = pl.BlockSpec(memory_space=pltpu.VMEM)
SMEM = pl.BlockSpec(memory_space=pltpu.SMEM)
HBM = pl.BlockSpec(memory_space=pltpu.HBM)


def head_row(values):
    lane = lax.broadcasted_iota(jnp.int32, (HEAD, PAIR), 1)
    row = jnp.zeros((HEAD, PAIR), jnp.float32)
    for n, value in enumerate(values):
        row = jnp.where(lane == n, value.astype(jnp.float32), row)
    return row.astype(jnp.bfloat16)


def pack_kernel(a_cols, p_cols, a_blocks, p_blocks, a_out, p_out):
    a_head = head_row([a_cols[0, s, j, k] for s in range(SEC) for j in range(OWN) for k in range(KS)])
    p_head = head_row([p_cols[0, s, 0, j, q] for s in range(SEC) for j in range(OWN) for q in range(KP)])
    for n in range(a_out.shape[0]):
        a_out[n, :BODY, :] = a_blocks[...]
        a_out[n, BODY:, :] = jnp.zeros((HEAD, KS * BLK), jnp.bfloat16)
        a_out[n, BODY:, :PAIR] = a_head
    p_out[:BODY, :] = p_blocks[...]
    p_out[BODY:, :] = jnp.zeros((HEAD, KP * BLK), jnp.bfloat16)
    p_out[BODY:, :PAIR] = p_head


def twins(two):
    turned = pltpu.roll(two, BLK, 1)
    low = lax.broadcasted_iota(jnp.int32, two.shape, 1) < BLK
    return jnp.where(low, two, turned), jnp.where(low, turned, two)


def copies_of(tile):
    found = []
    for t in range(tile.shape[1] // PAIR):
        found.extend(twins(tile[:, t * PAIR : (t + 1) * PAIR].astype(jnp.float32)))
    return found


def swap(tile):
    return jnp.concatenate([tile[:, BLK:], tile[:, :BLK]], axis=1)


def masks_of(head, first, count, pairs):
    half = lax.broadcasted_iota(jnp.int32, (STEP, PAIR), 1) // BLK
    cols = [jnp.broadcast_to(head[:, first + n : first + n + 1], (STEP, PAIR)) for n in range(count)]
    return [[(half + 2 * pair).astype(jnp.float32) == col for col in cols] for pair in pairs]


def source_of(shift, axis):
    size = lax.axis_size(axis)
    return lax.rem(lax.axis_index(axis) - shift + size, size)


def expand_kernel(*refs):
    p_parts, (wide, held, sems) = refs[:HALF], refs[HALF:]
    copies = [pltpu.make_async_copy(part, held.at[n], sems.at[n]) for n, part in enumerate(p_parts)]
    for copy in copies:
        copy.start()
    for place, copy in enumerate(copies):
        copy.wait()
        head = held[place, BODY:, :PAIR].astype(jnp.float32)
        for n in range(SEC * OWN):
            s, j = n // OWN, n % OWN
            masks = masks_of(head, n * KP, KP, range(NCC // 2))
            slab = ((s * HALF + place) * OWN + j) * BLK
            for g in range(BLK // STEP):
                copies_in = copies_of(held[place, n * BLK + g * STEP : n * BLK + (g + 1) * STEP, :])
                for pair in range(NCC // 2):
                    acc = jnp.where(masks[pair][0], copies_in[0], 0.0)
                    for q in range(1, KP):
                        acc = jnp.where(masks[pair][q], copies_in[q], acc)
                    first = slab + g * STEP
                    wide[first : first + STEP, pair * PAIR : (pair + 1) * PAIR] = acc.astype(jnp.bfloat16)


def gather_rows(a_ref, rows):
    sources = [source_of(shift, "row") for shifts in SHIFTS for shift in shifts]
    for src in range(a_ref.shape[0]):
        head = a_ref[src, BODY:, :PAIR].astype(jnp.float32)
        for j in range(OWN):
            row = src * BLK
            for s in range(SEC):
                masks = masks_of(head, (s * OWN + j) * KS, KS, sources)
                for g in range(BLK // STEP):
                    first = (s * OWN + j) * BLK + g * STEP
                    copies = copies_of(a_ref[src, first : first + STEP, :])
                    for pair in range(IBS // OWN):
                        acc = jnp.where(masks[pair][0], copies[0], 0.0)
                        for k in range(1, KS):
                            acc = acc + jnp.where(masks[pair][k], copies[k], 0.0)
                        lane = ((pair // HALF * SEC + s) * HALF + pair % HALF) * PAIR
                        rows[j, row + g * STEP : row + (g + 1) * STEP, lane : lane + PAIR] = acc.astype(jnp.bfloat16)


def all_rows(rows_own, a_other, rows):
    rows[0] = rows_own[...]
    gather_rows(a_other, rows.at[1])


def product_kernel(near, turn, c_cols, rows, wide_first, wide_second, out, full):
    core, layer = lax.axis_index("core"), lax.axis_index("layer")
    place = lax.rem(layer, near) ^ turn
    owner, j = place // OWN, lax.rem(place, OWN)
    side = jnp.where(owner == core, 0, 1)
    wide = jnp.concatenate([wide_first[...], wide_second[...]], axis=0)
    full[...] = jnp.dot(rows[side, j], wide, preferred_element_type=jnp.float32).astype(jnp.bfloat16)
    low = lax.broadcasted_iota(jnp.int32, (BLK, PAIR), 1).astype(jnp.int16) < jnp.int16(BLK)
    for n in range(out.shape[0]):
        i = n * near + place
        for pair in range(KC // 2):
            picked = []
            for m in range(2):
                c = c_cols[0, pair * 2 + m, i]
                two = full[n * BLK : (n + 1) * BLK, pl.ds(pl.multiple_of(c // 2 * PAIR, PAIR), PAIR)]
                picked.append(jnp.where(lax.rem(c, 2) == m, two, swap(two)))
            out[n, :, pair * PAIR : (pair + 1) * PAIR] = jnp.where(low, *picked)


def local(a_blocks, a_cols, p_blocks, p_cols, c_cols):
    rows, chips, layers = lax.axis_size("row"), lax.axis_size("chip"), lax.axis_size("layer")
    near = 4
    a_out, p_out = pl.pallas_call(
        pack_kernel,
        out_shape=(
            jax.ShapeDtypeStruct((chips, BODY + HEAD, KS * BLK), jnp.bfloat16),
            jax.ShapeDtypeStruct((BODY + HEAD, KP * BLK), jnp.bfloat16),
        ),
        in_specs=[SMEM, SMEM, VMEM, VMEM],
        out_specs=(VMEM, VMEM),
    )(a_cols, p_cols, a_blocks.reshape(BODY, KS * BLK), p_blocks.reshape(BODY, KP * BLK))

    def expand(*parts):
        return pl.pallas_call(
            expand_kernel,
            out_shape=jax.ShapeDtypeStruct((HALF * SEC * OWN * BLK, NCC * BLK), jnp.bfloat16),
            in_specs=[HBM] * HALF,
            out_specs=VMEM,
            scratch_shapes=[
                pltpu.VMEM((HALF, BODY + HEAD, KP * BLK), jnp.bfloat16),
                pltpu.SemaphoreType.DMA((HALF,)),
            ],
            cost_estimate=pl.CostEstimate(flops=10**6, bytes_accessed=2 * 10**6, transcendentals=0),
            compiler_params=pltpu.CompilerParams(vmem_limit_bytes=SMALL),
        )(*parts)

    a_own = lax.all_to_all(a_out, "chip", 0, 0, tiled=True)
    p_parts = [p_out] + [lax.ppermute(p_out, "row", [(i, (i + d) % rows) for i in range(rows)]) for d in range(1, rows)]
    first = expand(*[p_parts[d] for d in SHIFTS[0]])
    a_other = lax.ppermute(a_own, "core", [(0, 1), (1, 0)])
    rows_own = pl.pallas_call(
        gather_rows,
        out_shape=jax.ShapeDtypeStruct((OWN, chips * BLK, SEC * IBS * BLK), jnp.bfloat16),
        in_specs=[VMEM],
        out_specs=VMEM,
        cost_estimate=pl.CostEstimate(flops=10**6, bytes_accessed=2 * 10**6, transcendentals=0),
        compiler_params=pltpu.CompilerParams(vmem_limit_bytes=SMALL),
    )(a_own)
    second = expand(*[p_parts[d] for d in SHIFTS[1]])
    rows_all = pl.pallas_call(
        all_rows,
        out_shape=jax.ShapeDtypeStruct((CORES,) + rows_own.shape, jnp.bfloat16),
        in_specs=[VMEM, VMEM],
        out_specs=VMEM,
        cost_estimate=pl.CostEstimate(flops=10**6, bytes_accessed=4 * 10**6, transcendentals=0),
        compiler_params=pltpu.CompilerParams(vmem_limit_bytes=SMALL),
    )(rows_own, a_other)

    def product(turn):
        return pl.pallas_call(
            lambda *refs: product_kernel(near, turn, *refs),
            out_shape=jax.ShapeDtypeStruct((layers // near, BLK, KC * BLK), jnp.bfloat16),
            in_specs=[SMEM] + [VMEM] * 3,
            out_specs=VMEM,
            scratch_shapes=[pltpu.VMEM((chips * BLK, NCC * BLK), jnp.bfloat16)],
            cost_estimate=pl.CostEstimate(flops=5 * 10**8, bytes_accessed=3 * 10**6, transcendentals=0),
            compiler_params=pltpu.CompilerParams(vmem_limit_bytes=2 * SMALL),
        )(c_cols.transpose(0, 2, 1), rows_all, first, second)

    def partners(turn):
        pairs = []
        for core in range(CORES):
            for n in range(layers):
                start = near // 2 * core
                to = n // near * near + (n % near ^ turn)
                pairs.append((core * layers + (n + start) % layers, core * layers + (to + start) % layers))
        return pairs

    sums = []
    for turn in range(near - 1, 0, -1):
        sent = product(turn)
        sums.append(lax.ppermute(sent, ("core", "layer"), partners(turn)))
    sums.append(product(0))
    part = sum(v.astype(jnp.float32) for v in sums).astype(jnp.bfloat16)
    far = [[o + near * g for g in range(layers // near)] for o in range(near)]
    got = lax.all_to_all(part, "layer", 0, 0, axis_index_groups=far, tiled=True)
    return got.astype(jnp.float32).sum(axis=0).astype(jnp.bfloat16)[None, None]


def solution(mesh):
    rows, cols, layers = mesh.devices.shape
    split = jax.sharding.Mesh(
        mesh.devices.reshape(rows, cols // CORES, CORES, layers), ("row", "chip", "core", "layer")
    )
    col = ("chip", "core")
    return jax.shard_map(
        local,
        mesh=split,
        in_specs=(
            P("layer", None, ("row",) + col, None, None),
            P("layer", None, ("row",) + col, None),
            P("layer", None, col, "row", None, None),
            P("layer", None, col, "row", None),
            P(col, "row", None),
        ),
        out_specs=P(col, ("row", "layer"), None, None),
        check_vma=False,
    )
```

```python
import jax
import jax.numpy as jnp
from jax import lax
from jax.experimental import pallas as pl
from jax.experimental.pallas import tpu as pltpu
from jax.sharding import PartitionSpec as P


BLK = 64
KS = 8
KP = 4
KC = 8
NCC = 16
SEC = 2
OWN = 2
IBS = 8
CORES = 2
HEAD = 16
BODY = SEC * OWN * BLK
PAIR = 2 * BLK
SMALL = 8 * 1024 * 1024
SHIFTS = ((0, 3), (2, 1))
HALF = 2
STEP = 16
VMEM = pl.BlockSpec(memory_space=pltpu.VMEM)
SMEM = pl.BlockSpec(memory_space=pltpu.SMEM)
HBM = pl.BlockSpec(memory_space=pltpu.HBM)


def head_row(values):
    lane = lax.broadcasted_iota(jnp.int32, (HEAD, PAIR), 1)
    row = jnp.zeros((HEAD, PAIR), jnp.float32)
    for n, value in enumerate(values):
        row = jnp.where(lane == n, value.astype(jnp.float32), row)
    return row.astype(jnp.bfloat16)


def pack_a_kernel(a_cols, a_blocks, a_out):
    head = head_row([a_cols[0, s, j, k] for s in range(SEC) for j in range(OWN) for k in range(KS)])
    for n in range(a_out.shape[0]):
        a_out[n, :BODY, :] = a_blocks[...]
        a_out[n, BODY:, :] = jnp.zeros((HEAD, KS * BLK), jnp.bfloat16)
        a_out[n, BODY:, :PAIR] = head


def pack_p_kernel(p_cols, p_blocks, p_out):
    head = head_row([p_cols[0, s, 0, j, q] for s in range(SEC) for j in range(OWN) for q in range(KP)])
    p_out[:BODY, :] = p_blocks[...]
    p_out[BODY:, :] = jnp.zeros((HEAD, KP * BLK), jnp.bfloat16)
    p_out[BODY:, :PAIR] = head


def twins(two):
    turned = pltpu.roll(two, BLK, 1)
    low = lax.broadcasted_iota(jnp.int32, two.shape, 1) < BLK
    return jnp.where(low, two, turned), jnp.where(low, turned, two)


def copies_of(tile):
    found = []
    for t in range(tile.shape[1] // PAIR):
        found.extend(twins(tile[:, t * PAIR : (t + 1) * PAIR].astype(jnp.float32)))
    return found


def swap(tile):
    return jnp.concatenate([tile[:, BLK:], tile[:, :BLK]], axis=1)


def masks_of(head, first, count, pairs):
    half = lax.broadcasted_iota(jnp.int32, (STEP, PAIR), 1) // BLK
    cols = [jnp.broadcast_to(head[:, first + n : first + n + 1], (STEP, PAIR)) for n in range(count)]
    return [[(half + 2 * pair).astype(jnp.float32) == col for col in cols] for pair in pairs]


def source_of(shift, axis):
    size = lax.axis_size(axis)
    return lax.rem(lax.axis_index(axis) - shift + size, size)


def expand_kernel(*refs):
    p_parts, (wide, held, sems) = refs[:HALF], refs[HALF:]
    copies = [pltpu.make_async_copy(part, held.at[n], sems.at[n]) for n, part in enumerate(p_parts)]
    for copy in copies:
        copy.start()
    for place, copy in enumerate(copies):
        copy.wait()
        head = held[place, BODY:, :PAIR].astype(jnp.float32)
        for n in range(SEC * OWN):
            s, j = n // OWN, n % OWN
            masks = masks_of(head, n * KP, KP, range(NCC // 2))
            slab = ((s * HALF + place) * OWN + j) * BLK
            for g in range(BLK // STEP):
                copies_in = copies_of(held[place, n * BLK + g * STEP : n * BLK + (g + 1) * STEP, :])
                for pair in range(NCC // 2):
                    acc = jnp.where(masks[pair][0], copies_in[0], 0.0)
                    for q in range(1, KP):
                        acc = jnp.where(masks[pair][q], copies_in[q], acc)
                    first = slab + g * STEP
                    wide[first : first + STEP, pair * PAIR : (pair + 1) * PAIR] = acc.astype(jnp.bfloat16)


def gather_rows(a_ref, rows):
    sources = [source_of(shift, "row") for shifts in SHIFTS for shift in shifts]
    half = lax.broadcasted_iota(jnp.int32, (STEP, PAIR), 1) // BLK
    low = half.astype(jnp.int16) < jnp.int16(1)
    none = jnp.zeros((STEP, PAIR), jnp.bfloat16)
    for src in range(a_ref.shape[0]):
        head = a_ref[src, BODY:, :PAIR].astype(jnp.float32)
        for j in range(OWN):
            row = src * BLK
            for s in range(SEC):
                at = (s * OWN + j) * KS
                cols = [jnp.broadcast_to(head[:, at + k : at + k + 1], (STEP, PAIR)) for k in range(KS)]
                cols = [col.astype(jnp.int32).astype(jnp.int16) for col in cols]
                masks = [[(half + 2 * pair).astype(jnp.int16) == col for col in cols] for pair in sources]
                for g in range(BLK // STEP):
                    first = (s * OWN + j) * BLK + g * STEP
                    copies = []
                    for t in range(KS // 2):
                        two = a_ref[src, first : first + STEP, t * PAIR : (t + 1) * PAIR]
                        copies += [jnp.where(low, two, swap(two)), jnp.where(low, swap(two), two)]
                    for pair in range(IBS // OWN):
                        acc = jnp.where(masks[pair][0], copies[0], none)
                        for k in range(1, KS):
                            acc = acc + jnp.where(masks[pair][k], copies[k], none)
                        lane = ((pair // HALF * SEC + s) * HALF + pair % HALF) * PAIR
                        rows[j, row + g * STEP : row + (g + 1) * STEP, lane : lane + PAIR] = acc


def all_rows(rows_own, a_other, rows):
    rows[0] = rows_own[...]
    gather_rows(a_other, rows.at[1])


def product_kernel(near, turn, c_cols, rows, wide_first, wide_second, out, full):
    core, layer = lax.axis_index("core"), lax.axis_index("layer")
    place = lax.rem(layer, near) ^ turn
    owner, j = place // OWN, lax.rem(place, OWN)
    side = jnp.where(owner == core, 0, 1)
    wide = jnp.concatenate([wide_first[...], wide_second[...]], axis=0)
    full[...] = jnp.dot(rows[side, j], wide, preferred_element_type=jnp.float32).astype(jnp.bfloat16)
    low = lax.broadcasted_iota(jnp.int32, (BLK, PAIR), 1).astype(jnp.int16) < jnp.int16(BLK)
    for n in range(out.shape[0]):
        i = n * near + place
        for pair in range(KC // 2):
            picked = []
            for m in range(2):
                c = c_cols[0, pair * 2 + m, i]
                two = full[n * BLK : (n + 1) * BLK, pl.ds(pl.multiple_of(c // 2 * PAIR, PAIR), PAIR)]
                picked.append(jnp.where(lax.rem(c, 2) == m, two, swap(two)))
            out[n, :, pair * PAIR : (pair + 1) * PAIR] = jnp.where(low, *picked)


def local(a_blocks, a_cols, p_blocks, p_cols, c_cols):
    rows, chips, layers = lax.axis_size("row"), lax.axis_size("chip"), lax.axis_size("layer")
    near = 4
    a_out = pl.pallas_call(
        pack_a_kernel,
        out_shape=jax.ShapeDtypeStruct((chips, BODY + HEAD, KS * BLK), jnp.bfloat16),
        in_specs=[SMEM, VMEM],
        out_specs=VMEM,
    )(a_cols, a_blocks.reshape(BODY, KS * BLK))
    p_out = pl.pallas_call(
        pack_p_kernel,
        out_shape=jax.ShapeDtypeStruct((BODY + HEAD, KP * BLK), jnp.bfloat16),
        in_specs=[SMEM, VMEM],
        out_specs=VMEM,
    )(p_cols, p_blocks.reshape(BODY, KP * BLK))

    def expand(*parts):
        return pl.pallas_call(
            expand_kernel,
            out_shape=jax.ShapeDtypeStruct((HALF * SEC * OWN * BLK, NCC * BLK), jnp.bfloat16),
            in_specs=[HBM] * HALF,
            out_specs=VMEM,
            scratch_shapes=[
                pltpu.VMEM((HALF, BODY + HEAD, KP * BLK), jnp.bfloat16),
                pltpu.SemaphoreType.DMA((HALF,)),
            ],
            cost_estimate=pl.CostEstimate(flops=10**6, bytes_accessed=2 * 10**6, transcendentals=0),
            compiler_params=pltpu.CompilerParams(vmem_limit_bytes=SMALL),
        )(*parts)

    a_own = lax.all_to_all(a_out, "chip", 0, 0, tiled=True)
    p_parts = [p_out] + [lax.ppermute(p_out, "row", [(i, (i + d) % rows) for i in range(rows)]) for d in range(1, rows)]
    first = expand(*[p_parts[d] for d in SHIFTS[0]])
    a_other = lax.ppermute(a_own, "core", [(0, 1), (1, 0)])
    rows_own = pl.pallas_call(
        gather_rows,
        out_shape=jax.ShapeDtypeStruct((OWN, chips * BLK, SEC * IBS * BLK), jnp.bfloat16),
        in_specs=[VMEM],
        out_specs=VMEM,
        cost_estimate=pl.CostEstimate(flops=10**6, bytes_accessed=2 * 10**6, transcendentals=0),
        compiler_params=pltpu.CompilerParams(vmem_limit_bytes=SMALL),
    )(a_own)
    second = expand(*[p_parts[d] for d in SHIFTS[1]])
    rows_all = pl.pallas_call(
        all_rows,
        out_shape=jax.ShapeDtypeStruct((CORES,) + rows_own.shape, jnp.bfloat16),
        in_specs=[VMEM, VMEM],
        out_specs=VMEM,
        cost_estimate=pl.CostEstimate(flops=10**6, bytes_accessed=4 * 10**6, transcendentals=0),
        compiler_params=pltpu.CompilerParams(vmem_limit_bytes=SMALL),
    )(rows_own, a_other)

    def product(turn):
        return pl.pallas_call(
            lambda *refs: product_kernel(near, turn, *refs),
            out_shape=jax.ShapeDtypeStruct((layers // near, BLK, KC * BLK), jnp.bfloat16),
            in_specs=[SMEM] + [VMEM] * 3,
            out_specs=VMEM,
            scratch_shapes=[pltpu.VMEM((chips * BLK, NCC * BLK), jnp.bfloat16)],
            cost_estimate=pl.CostEstimate(flops=5 * 10**8, bytes_accessed=3 * 10**6, transcendentals=0),
            compiler_params=pltpu.CompilerParams(vmem_limit_bytes=2 * SMALL),
        )(c_cols.transpose(0, 2, 1), rows_all, first, second)

    def partners(turn):
        pairs = []
        for core in range(CORES):
            for n in range(layers):
                start = near // 2 * core
                to = n // near * near + (n % near ^ turn)
                pairs.append((core * layers + (n + start) % layers, core * layers + (to + start) % layers))
        return pairs

    sums = []
    for turn in range(near - 1, 0, -1):
        sent = product(turn)
        sums.append(lax.ppermute(sent, ("core", "layer"), partners(turn)))
    sums.append(product(0))
    part = sum(v.astype(jnp.float32) for v in sums).astype(jnp.bfloat16)
    far = [[o + near * g for g in range(layers // near)] for o in range(near)]
    got = lax.all_to_all(part, "layer", 0, 0, axis_index_groups=far, tiled=True)
    return got.astype(jnp.float32).sum(axis=0).astype(jnp.bfloat16)[None, None]


def solution(mesh):
    rows, cols, layers = mesh.devices.shape
    split = jax.sharding.Mesh(
        mesh.devices.reshape(rows, cols // CORES, CORES, layers), ("row", "chip", "core", "layer")
    )
    col = ("chip", "core")
    return jax.shard_map(
        local,
        mesh=split,
        in_specs=(
            P("layer", None, ("row",) + col, None, None),
            P("layer", None, ("row",) + col, None),
            P("layer", None, col, "row", None, None),
            P("layer", None, col, "row", None),
            P(col, "row", None),
        ),
        out_specs=P(col, ("row", "layer"), None, None),
        check_vma=False,
    )
```

```python
import jax
import jax.numpy as jnp
from jax import lax
from jax.experimental import pallas as pl
from jax.experimental.pallas import tpu as pltpu
from jax.sharding import PartitionSpec as P


BLK = 64
KS = 8
KP = 4
KC = 8
NCC = 16
SEC = 2
OWN = 2
IBS = 8
CORES = 2
HEAD = 16
BODY = SEC * OWN * BLK
PAIR = 2 * BLK
SMALL = 8 * 1024 * 1024
SHIFTS = ((0, 3), (2, 1))
HALF = 2
STEP = 16
VMEM = pl.BlockSpec(memory_space=pltpu.VMEM)
SMEM = pl.BlockSpec(memory_space=pltpu.SMEM)
HBM = pl.BlockSpec(memory_space=pltpu.HBM)


def head_row(values):
    lane = lax.broadcasted_iota(jnp.int32, (HEAD, PAIR), 1)
    row = jnp.zeros((HEAD, PAIR), jnp.float32)
    for n, value in enumerate(values):
        row = jnp.where(lane == n, value.astype(jnp.float32), row)
    return row.astype(jnp.bfloat16)


def pack_a_kernel(a_cols, a_blocks, a_out):
    head = head_row([a_cols[0, s, j, k] for s in range(SEC) for j in range(OWN) for k in range(KS)])
    for n in range(a_out.shape[0]):
        a_out[n, :BODY, :] = a_blocks[...]
        a_out[n, BODY:, :] = jnp.zeros((HEAD, KS * BLK), jnp.bfloat16)
        a_out[n, BODY:, :PAIR] = head


def pack_p_kernel(p_cols, p_blocks, p_out):
    head = head_row([p_cols[0, s, 0, j, q] for s in range(SEC) for j in range(OWN) for q in range(KP)])
    p_out[:BODY, :] = p_blocks[...]
    p_out[BODY:, :] = jnp.zeros((HEAD, KP * BLK), jnp.bfloat16)
    p_out[BODY:, :PAIR] = head


def swap(tile):
    return jnp.concatenate([tile[:, BLK:], tile[:, :BLK]], axis=1)


def copies_of(tile):
    low = lax.broadcasted_iota(jnp.int32, (STEP, PAIR), 1).astype(jnp.int16) < jnp.int16(BLK)
    found = []
    for t in range(tile.shape[1] // PAIR):
        two = tile[:, t * PAIR : (t + 1) * PAIR]
        found += [jnp.where(low, two, swap(two)), jnp.where(low, swap(two), two)]
    return found


def masks_of(head, first, count, pairs):
    half = lax.broadcasted_iota(jnp.int32, (STEP, PAIR), 1) // BLK
    cols = [jnp.broadcast_to(head[:, first + n : first + n + 1], (STEP, PAIR)) for n in range(count)]
    cols = [col.astype(jnp.int32).astype(jnp.int16) for col in cols]
    return [[(half + 2 * pair).astype(jnp.int16) == col for col in cols] for pair in pairs]


def source_of(shift, axis):
    size = lax.axis_size(axis)
    return lax.rem(lax.axis_index(axis) - shift + size, size)


def expand_kernel(*refs):
    p_parts, (wide, held, sems) = refs[:HALF], refs[HALF:]
    copies = [pltpu.make_async_copy(part, held.at[n], sems.at[n]) for n, part in enumerate(p_parts)]
    for copy in copies:
        copy.start()
    for place, copy in enumerate(copies):
        copy.wait()
        head = held[place, BODY:, :PAIR].astype(jnp.float32)
        for n in range(SEC * OWN):
            s, j = n // OWN, n % OWN
            masks = masks_of(head, n * KP, KP, range(NCC // 2))
            slab = ((s * HALF + place) * OWN + j) * BLK
            for g in range(BLK // STEP):
                copies_in = copies_of(held[place, n * BLK + g * STEP : n * BLK + (g + 1) * STEP, :])
                for pair in range(NCC // 2):
                    acc = jnp.zeros((STEP, PAIR), jnp.bfloat16)
                    for q in range(KP):
                        acc = jnp.where(masks[pair][q], copies_in[q], acc)
                    first = slab + g * STEP
                    wide[first : first + STEP, pair * PAIR : (pair + 1) * PAIR] = acc


def gather_rows(a_ref, rows):
    sources = [source_of(shift, "row") for shifts in SHIFTS for shift in shifts]
    none = jnp.zeros((STEP, PAIR), jnp.bfloat16)
    for src in range(a_ref.shape[0]):
        head = a_ref[src, BODY:, :PAIR].astype(jnp.float32)
        for j in range(OWN):
            row = src * BLK
            for s in range(SEC):
                masks = masks_of(head, (s * OWN + j) * KS, KS, sources)
                for g in range(BLK // STEP):
                    first = (s * OWN + j) * BLK + g * STEP
                    copies = copies_of(a_ref[src, first : first + STEP, :])
                    for pair in range(IBS // OWN):
                        acc = jnp.where(masks[pair][0], copies[0], none)
                        for k in range(1, KS):
                            acc = acc + jnp.where(masks[pair][k], copies[k], none)
                        lane = ((pair // HALF * SEC + s) * HALF + pair % HALF) * PAIR
                        rows[j, row + g * STEP : row + (g + 1) * STEP, lane : lane + PAIR] = acc


def all_rows(rows_own, a_other, rows):
    rows[0] = rows_own[...]
    gather_rows(a_other, rows.at[1])


def product_kernel(near, turn, c_cols, rows, wide_first, wide_second, out, full):
    core, layer = lax.axis_index("core"), lax.axis_index("layer")
    place = lax.rem(layer, near) ^ turn
    owner, j = place // OWN, lax.rem(place, OWN)
    side = jnp.where(owner == core, 0, 1)
    wide = jnp.concatenate([wide_first[...], wide_second[...]], axis=0)
    full[...] = jnp.dot(rows[side, j], wide, preferred_element_type=jnp.float32).astype(jnp.bfloat16)
    low = lax.broadcasted_iota(jnp.int32, (BLK, PAIR), 1).astype(jnp.int16) < jnp.int16(BLK)
    for n in range(out.shape[0]):
        i = n * near + place
        for pair in range(KC // 2):
            picked = []
            for m in range(2):
                c = c_cols[0, pair * 2 + m, i]
                two = full[n * BLK : (n + 1) * BLK, pl.ds(pl.multiple_of(c // 2 * PAIR, PAIR), PAIR)]
                picked.append(jnp.where(lax.rem(c, 2) == m, two, swap(two)))
            out[n, :, pair * PAIR : (pair + 1) * PAIR] = jnp.where(low, *picked)


def local(a_blocks, a_cols, p_blocks, p_cols, c_cols):
    rows, chips, layers = lax.axis_size("row"), lax.axis_size("chip"), lax.axis_size("layer")
    near = 4
    a_out = pl.pallas_call(
        pack_a_kernel,
        out_shape=jax.ShapeDtypeStruct((chips, BODY + HEAD, KS * BLK), jnp.bfloat16),
        in_specs=[SMEM, VMEM],
        out_specs=VMEM,
    )(a_cols, a_blocks.reshape(BODY, KS * BLK))
    p_out = pl.pallas_call(
        pack_p_kernel,
        out_shape=jax.ShapeDtypeStruct((BODY + HEAD, KP * BLK), jnp.bfloat16),
        in_specs=[SMEM, VMEM],
        out_specs=VMEM,
        compiler_params=pltpu.CompilerParams(vmem_limit_bytes=SMALL),
    )(p_cols, p_blocks.reshape(BODY, KP * BLK))

    def expand(*parts):
        return pl.pallas_call(
            expand_kernel,
            out_shape=jax.ShapeDtypeStruct((HALF * SEC * OWN * BLK, NCC * BLK), jnp.bfloat16),
            in_specs=[HBM] * HALF,
            out_specs=VMEM,
            scratch_shapes=[
                pltpu.VMEM((HALF, BODY + HEAD, KP * BLK), jnp.bfloat16),
                pltpu.SemaphoreType.DMA((HALF,)),
            ],
            cost_estimate=pl.CostEstimate(flops=10**6, bytes_accessed=2 * 10**6, transcendentals=0),
            compiler_params=pltpu.CompilerParams(vmem_limit_bytes=SMALL),
        )(*parts)

    a_own = lax.all_to_all(a_out, "chip", 0, 0, tiled=True)
    p_parts = [p_out] + [lax.ppermute(p_out, "row", [(i, (i + d) % rows) for i in range(rows)]) for d in range(1, rows)]
    first = expand(*[p_parts[d] for d in SHIFTS[0]])
    a_other = lax.ppermute(a_own, "core", [(0, 1), (1, 0)])
    rows_own = pl.pallas_call(
        gather_rows,
        out_shape=jax.ShapeDtypeStruct((OWN, chips * BLK, SEC * IBS * BLK), jnp.bfloat16),
        in_specs=[VMEM],
        out_specs=VMEM,
        cost_estimate=pl.CostEstimate(flops=10**6, bytes_accessed=2 * 10**6, transcendentals=0),
        compiler_params=pltpu.CompilerParams(vmem_limit_bytes=SMALL),
    )(a_own)
    second = expand(*[p_parts[d] for d in SHIFTS[1]])
    rows_all = pl.pallas_call(
        all_rows,
        out_shape=jax.ShapeDtypeStruct((CORES,) + rows_own.shape, jnp.bfloat16),
        in_specs=[VMEM, VMEM],
        out_specs=VMEM,
        cost_estimate=pl.CostEstimate(flops=10**6, bytes_accessed=4 * 10**6, transcendentals=0),
        compiler_params=pltpu.CompilerParams(vmem_limit_bytes=SMALL),
    )(rows_own, a_other)

    def product(turn):
        return pl.pallas_call(
            lambda *refs: product_kernel(near, turn, *refs),
            out_shape=jax.ShapeDtypeStruct((layers // near, BLK, KC * BLK), jnp.bfloat16),
            in_specs=[SMEM] + [VMEM] * 3,
            out_specs=VMEM,
            scratch_shapes=[pltpu.VMEM((chips * BLK, NCC * BLK), jnp.bfloat16)],
            cost_estimate=pl.CostEstimate(flops=5 * 10**8, bytes_accessed=3 * 10**6, transcendentals=0),
            compiler_params=pltpu.CompilerParams(vmem_limit_bytes=2 * SMALL),
        )(c_cols.transpose(0, 2, 1), rows_all, first, second)

    def partners(turn):
        pairs = []
        for core in range(CORES):
            for n in range(layers):
                start = near // 2 * core
                to = n // near * near + (n % near ^ turn)
                pairs.append((core * layers + (n + start) % layers, core * layers + (to + start) % layers))
        return pairs

    sums = []
    for turn in range(near - 1, 0, -1):
        sent = product(turn)
        sums.append(lax.ppermute(sent, ("core", "layer"), partners(turn)))
    sums.append(product(0))
    part = sum(v.astype(jnp.float32) for v in sums).astype(jnp.bfloat16)
    far = [[o + near * g for g in range(layers // near)] for o in range(near)]
    got = lax.all_to_all(part, "layer", 0, 0, axis_index_groups=far, tiled=True)
    return got.astype(jnp.float32).sum(axis=0).astype(jnp.bfloat16)[None, None]


def solution(mesh):
    rows, cols, layers = mesh.devices.shape
    split = jax.sharding.Mesh(
        mesh.devices.reshape(rows, cols // CORES, CORES, layers), ("row", "chip", "core", "layer")
    )
    col = ("chip", "core")
    return jax.shard_map(
        local,
        mesh=split,
        in_specs=(
            P("layer", None, ("row",) + col, None, None),
            P("layer", None, ("row",) + col, None),
            P("layer", None, col, "row", None, None),
            P("layer", None, col, "row", None),
            P(col, "row", None),
        ),
        out_specs=P(col, ("row", "layer"), None, None),
        check_vma=False,
    )
```
